32 devices in a mesh: groups: 2 (over x), span: 16 (over z, y, core).
Axes of the slice: x: 2, y: 2, z: 4, core: 2. Of those that a mesh axis runs over, the one named last changes fastest.
Arguments:
- hidden_in: bfloat16 [16384, 2240], P(('groups', 'span')), parts along dimension 0, may hold values from -16 to 16
- noisy_latents: float32 [16384, 32], P(('groups', 'span')), parts along dimension 0, may hold values from -6 to 6
- span_ids: int32 [16384], P(('groups', 'span')), parts along dimension 0, may hold values from 0 to 31, as said below
- tile_map: int32 [16384], P('groups'), parts along dimension 0, may hold values from 0 to 8191, as said below
- qkv_weight: bfloat16 [2240, 3360], replicated, may hold values from -0.125 to 0.125
- out_weight: bfloat16 [1120, 2240], replicated, may hold values from -0.1875 to 0.1875
- norm_gain: float32 [2240], replicated, may hold values from 0.1 to 1.9
- velocity_weight: bfloat16 [2240, 32], replicated, may hold values from -0.125 to 0.125
- conv_first: bfloat16 [3, 3, 32, 256], replicated, may hold values from -0.375 to 0.375
- conv_second: bfloat16 [3, 3, 256, 256], replicated, may hold values from -0.125 to 0.125
Outputs:
- new_latents: float32 [16384, 32], P(('groups', 'span')), parts along dimension 0
- decoded: bfloat16 [256, 64, 256], P(('groups', 'span')), parts along dimension 0
The draws below stay inside these ranges and needn't reach their ends.
There are 2 independent parts, one for each index of `groups`. The reference program is written for one: setup_inputs(seed, part) draws one part's arguments, and reference() takes and returns one part's arrays. A program takes and returns all parts, laid end to end along the dimension named above; an argument that names none is the same for every part. Nothing has to cross between parts.
Inputs may be any that keep to these rules, and one draw needn't show every extreme that they name: `span_ids`: never falling along the tokens; every span number occurs, each span holds 1 to 1024 tokens, and one span holds exactly 1024. `tile_map`: A permutation of the 8192 grid positions; the 512 tokens of each aligned block of tokens place exactly 32 tokens in each aligned block of 512 positions.
All inputs are finite; a program needn't handle non-finite values.
Results may differ from the reference program's by a relative error of at most 0.01.
Values may be sent and summed in bfloat16 or wider, within the bound.
A program may use at most 128 MiB of HBM per device.

```python
import math
import jax
import jax.numpy as jnp
from jax import lax

D = 2240
HEADS = 35
HDIM = 32
C = 32
CH = 256
IW = 64
TOK_DEV = 512
TOKENS = 8192
ROWS = 128
NSEG = 32
HD = 1120
N_SPAN = 16


def draw_hidden_in(key, part):
    key = jax.random.fold_in(key, 101)
    keys = jax.random.split(key, 4)
    scene_count = TOKENS // IW
    scene = jax.random.normal(keys[1], (scene_count, D), jnp.float32)
    scene_rows = jnp.repeat(scene, IW, axis=0)
    columns = jnp.exp(jax.random.uniform(keys[2], (D,), jnp.float32, math.log(0.3), math.log(3.0)))
    noise = jax.random.normal(keys[0], (TOKENS, D), jnp.float32)
    row_scale = jnp.exp(jax.random.uniform(keys[3], (TOKENS, 1), jnp.float32, math.log(0.1), math.log(1.0)))
    base = (0.7 * noise + 2.5 * scene_rows) * row_scale
    return jnp.clip(base * columns, -16.0, 16.0).astype(jnp.bfloat16)


def draw_span_ids(key, part):
    key = jax.random.fold_in(key, 303)
    long_key, extra_key, offset_key, align_key = jax.random.split(key, 4)
    devices = N_SPAN
    per_device = TOK_DEV
    long_dev = jax.random.randint(long_key, (), 1, min(4, devices - 2), jnp.int32)
    extra_dev = jax.random.randint(extra_key, (), 0, devices, jnp.int32)
    extra_dev = jnp.where((extra_dev == long_dev) | (extra_dev == long_dev + 1), (extra_dev + 2) % devices, extra_dev)
    offsets = jax.vmap(lambda single: jax.random.permutation(single, per_device - 1)[:3])(jax.random.split(offset_key, devices)).astype(jnp.int32) + 1
    device_no = jnp.arange(devices, dtype=jnp.int32)
    aligned = jax.random.randint(align_key, (devices,), 0, 2, jnp.int32)
    may_align = (device_no >= 1) & (device_no != long_dev + 2) & (aligned == 1)
    offsets = offsets.at[:, 0].set(jnp.where(may_align, 0, offsets[:, 0]))
    taken = jnp.where((device_no == long_dev) | (device_no == long_dev + 1), 0, jnp.where(device_no == extra_dev, 3, 2))
    used = jnp.arange(3, dtype=jnp.int32)[None, :] < taken[:, None]
    spots = jnp.where(used, device_no[:, None] * per_device + offsets, devices * per_device).astype(jnp.int32)
    starts = jnp.zeros((devices * per_device + 1,), jnp.int32).at[spots.reshape(-1)].set(1)
    bounds = jnp.stack([long_dev * per_device, (long_dev + 2) * per_device]).astype(jnp.int32)
    starts = starts.at[bounds].set(1)
    return jnp.cumsum(starts[:devices * per_device]).astype(jnp.int32)


def draw_tile_map(key, part):
    key = jax.random.fold_in(key, 202)
    send_key, recv_key = jax.random.split(key)
    count = N_SPAN
    block = TOK_DEV
    share = block // count
    sender = jax.vmap(lambda one: jax.random.permutation(one, block))(jax.random.split(send_key, count))
    receiver = jax.vmap(lambda one: jax.random.permutation(one, block))(jax.random.split(recv_key, count))
    source = jnp.arange(count, dtype=jnp.int32)[:, None, None]
    target = jnp.arange(count, dtype=jnp.int32)[None, :, None]
    within = jnp.arange(share, dtype=jnp.int32)[None, None, :]
    token = source * block + sender[source, target * share + within]
    place = target * block + receiver[target, source * share + within]
    result = jnp.zeros((count * block,), jnp.int32).at[token.reshape(-1)].set(place.reshape(-1).astype(jnp.int32))
    return result


def block_levels(own_key, shape, shards, low, largest):
    def one(axis_at, shards_of):
        steps = jax.random.uniform(jax.random.fold_in(jax.random.fold_in(own_key, 6), axis_at), (shards_of,), jnp.float32, low / len(shards), largest / len(shards))
        return jnp.repeat(jnp.exp(steps), shape[axis_at] // shards_of).reshape((-1,) + (1,) * (len(shape) - axis_at - 1))

    level = one(*shards[0])
    for cut in shards[1:]:
        level = level * one(*cut)
    return level


def centred(stream_key, shape, deviation, limit, pieces=(), kind=jnp.bfloat16):
    drawn = deviation * jax.random.normal(stream_key, shape, jnp.float32)
    if pieces:
        drawn = drawn * block_levels(stream_key, shape, pieces, -0.22, 0.18)
    return jnp.clip(drawn, -limit, limit).astype(kind)


def setup_inputs(seed: int = 0, part: int = 0) -> dict:
    streams_of = jax.random.split(jax.random.key(seed), 11)
    part_keys = jax.random.split(jax.random.fold_in(streams_of[10], part), 11)
    hidden_in = draw_hidden_in(jax.random.fold_in(jax.random.fold_in(streams_of[10], part), 71), part)
    noisy_latents = centred(part_keys[1], (TOKENS, C), 1.0, 6.0, ((0, 16),), jnp.float32)
    span_ids = draw_span_ids(jax.random.fold_in(jax.random.fold_in(streams_of[10], part), 71), part)
    tile_map = draw_tile_map(jax.random.fold_in(jax.random.fold_in(streams_of[10], part), 71), part)
    qkv_weight = centred(streams_of[4], (D, 3 * HD), D ** -0.5, 0.125)
    out_weight = centred(streams_of[5], (HD, D), HD ** -0.5, 0.1875)
    norm_gain = jnp.clip(1.0 + 0.18 * jax.random.normal(streams_of[6], (D,), jnp.float32), 0.1, 1.9)
    velocity_weight = centred(streams_of[7], (D, C), D ** -0.5, 0.125)
    conv_first = centred(streams_of[8], (3, 3, C, CH), (9 * C) ** -0.5, 0.375)
    conv_second = centred(streams_of[9], (3, 3, CH, CH), (9 * CH) ** -0.5, 0.125)
    return dict(hidden_in=hidden_in, noisy_latents=noisy_latents, span_ids=span_ids, tile_map=tile_map, qkv_weight=qkv_weight, out_weight=out_weight, norm_gain=norm_gain, velocity_weight=velocity_weight, conv_first=conv_first, conv_second=conv_second)


def conv_rows(padded, weight):
    height = padded.shape[0] - 2
    width = padded.shape[1]
    framed = jnp.pad(padded, ((0, 0), (1, 1), (0, 0)))
    patches = jnp.concatenate([framed[row_off:row_off + height, col_off:col_off + width, :] for row_off in range(3) for col_off in range(3)], axis=2)
    inputs = weight.shape[2]
    result = jnp.dot(patches.reshape(height * width, 9 * inputs), weight.reshape(9 * inputs, weight.shape[3]), preferred_element_type=jnp.float32)
    return result.reshape(height, width, weight.shape[3])

def reference(hidden_in, noisy_latents, span_ids, tile_map, qkv_weight, out_weight, norm_gain, velocity_weight, conv_first, conv_second):
    inner = HEADS * HDIM
    packed = jnp.dot(hidden_in, qkv_weight, preferred_element_type=jnp.float32).astype(jnp.bfloat16)
    query = jnp.maximum(packed[:, :inner], 0).reshape(TOKENS, HEADS, HDIM)
    keys = jnp.maximum(packed[:, inner:2 * inner], 0).reshape(TOKENS, HEADS, HDIM)
    values = packed[:, 2 * inner:].reshape(TOKENS, HEADS, HDIM)
    visible = (span_ids[None, :] <= jnp.arange(NSEG, dtype=jnp.int32)[:, None]).astype(jnp.float32)

    def one_head(operands):
        query_h, keys_h, values_h = operands
        query_f = query_h.astype(jnp.float32)
        keys_f = keys_h.astype(jnp.float32)
        values_f = values_h.astype(jnp.float32)
        outer = (keys_f[:, :, None] * values_f[:, None, :]).reshape(TOKENS, HDIM * HDIM)
        states = jnp.dot(visible, outer, precision=lax.Precision.HIGHEST).reshape(NSEG, HDIM, HDIM)
        sums = jnp.dot(visible, keys_f, precision=lax.Precision.HIGHEST)
        numer = jnp.einsum('td,tde->te', query_f, states[span_ids], precision=lax.Precision.HIGHEST)
        denom = 1.0 + lax.optimization_barrier(jnp.sum(query_f * sums[span_ids], axis=1))
        return numer / denom[:, None]
    heads_out = lax.map(one_head, (jnp.transpose(query, (1, 0, 2)), jnp.transpose(keys, (1, 0, 2)), jnp.transpose(values, (1, 0, 2))))
    attention = jnp.transpose(heads_out, (1, 0, 2)).reshape(TOKENS, inner).astype(jnp.bfloat16)
    mixed = hidden_in.astype(jnp.float32) + jnp.dot(attention, out_weight, preferred_element_type=jnp.float32)
    meansq = lax.optimization_barrier(jnp.mean(mixed * mixed, axis=1, keepdims=True))
    normed = (mixed * lax.rsqrt(meansq + 1e-06) * norm_gain).astype(jnp.bfloat16)
    velocity = jnp.dot(normed, velocity_weight, preferred_element_type=jnp.float32)
    new_latents = noisy_latents - 0.5 * velocity
    tile = jnp.zeros((TOKENS, C), jnp.bfloat16).at[tile_map].set(new_latents.astype(jnp.bfloat16)).reshape(ROWS, IW, C)
    padded = jnp.pad(tile, ((1, 1), (0, 0), (0, 0)))
    first = jax.nn.silu(conv_rows(padded, conv_first)).astype(jnp.bfloat16)
    decoded = conv_rows(jnp.pad(first, ((1, 1), (0, 0), (0, 0))), conv_second).astype(jnp.bfloat16)
    return (new_latents, decoded)
```

```python
import functools

import jax
import jax.numpy as jnp
from jax import lax
from jax.experimental import pallas as pl
from jax.experimental.pallas import tpu as pltpu
from jax.sharding import PartitionSpec as P

HDIM = 32
IW = 64
BLK = 256
LANE = 128
PER = LANE // HDIM
TEAM = 4
LAG = 3
AHEAD = 4
BF = jnp.bfloat16
F32 = jnp.float32


def dot(a, b):
    return jnp.dot(a, b, preferred_element_type=F32)


def dot_nt(a, b):
    return lax.dot_general(a, b, (((1,), (1,)), ((), ())), preferred_element_type=F32)


def iota(shape, axis):
    return lax.broadcasted_iota(jnp.int32, shape, axis)


def kernel(
    cfg,
    hid_hbm, noisy_hbm, span_hbm, map_hbm, wq_hbm, wo_hbm, gain_hbm, vw_hbm, w1_hbm, w2_hbm,
    lat_out, dec_out,
    noisy, span_ref, map_ref, gain, vw, w1,
    hidt, hid, wq, wo, w2, qt, kp, vt, numt, dent, keep, att, ybuf, vwt, vel,
    st_c0, st_b0, sum_c0, sum_b0, st_send, lead_send, lead_recv,
    part_recv, plane_send, plane_recv, fin_send, fin_recv, base, carry, after, onehot, xlat, outgoing, incoming,
    wide, halo_send, halo_recv, shifted,
    wsem, lsem, hsem, isem, psend, precv, gsend, grecv, fsend, frecv, lead_ssem, lead_rsem, asend, arecv, halo_ssem, halo_rsem,
):
    n, toks, d, inner = cfg
    me = lax.axis_index("span")
    mate = lax.rem(me, TEAM)
    team = me // TEAM
    teams = n // TEAM
    share = toks // n
    chunk = toks // 2
    lo = inner // BLK
    koff = inner - lo * BLK
    kw = kp.shape[1]
    tiles = kw // LANE
    units = st_send.shape[0]
    part = units // TEAM
    heads = inner // HDIM
    first_slot = koff // HDIM
    last_slot = first_slot + heads

    def remote(src, dst, ss, rs, dev):
        return pltpu.make_async_remote_copy(
            src_ref=src, dst_ref=dst, send_sem=ss, recv_sem=rs,
            device_id={"span": dev}, device_id_type=pl.DeviceIdType.MESH,
        )

    total = wq_hbm.shape[1]
    full = total // BLK
    rest = total - full * BLK

    def wcopy(b):
        cols = slice(b * BLK, min(b * BLK + BLK, total))
        return pltpu.make_async_copy(wq_hbm.at[:, cols], wq.at[:, cols], wsem.at[b])

    def hcopy(i):
        cols = pl.ds(i * LANE if isinstance(i, int) else pl.multiple_of(i * LANE, LANE), LANE)
        return pltpu.make_async_copy(hid_hbm.at[:, cols], hidt.at[:, cols], hsem.at[i])

    for i in range(toks // LANE):
        hcopy(i).start()
    smalls = [
        pltpu.make_async_copy(src, dst, isem.at[i])
        for i, (src, dst) in enumerate([
            (span_hbm, span_ref), (vw_hbm, vw), (map_hbm, map_ref), (noisy_hbm, noisy),
            (gain_hbm, gain), (w1_hbm, w1),
        ])
    ]
    for copy in smalls[:2]:
        copy.start()
    ocopy = pltpu.make_async_copy(wo_hbm, wo.at[koff : koff + inner], lsem.at[1])
    w2copy = pltpu.make_async_copy(w2_hbm, w2, lsem.at[2])
    pending = [wcopy(full)] if rest else []
    pending += [wcopy(b) for b in range(lo, full)] + smalls[2:] + [wcopy(b) for b in range(lo)] + [ocopy, w2copy]

    def fetch(count):
        for copy in pending[:count]:
            copy.start()
        del pending[:count]

    fetch(AHEAD)

    barrier = pltpu.get_barrier_semaphore()
    for k in range(1, n):
        pl.semaphore_signal(
            barrier, inc=1, device_id={"span": lax.rem(me + k, n)},
            device_id_type=pl.DeviceIdType.MESH,
        )

    def clear(ref, row0, row1, dtype):
        if row1 > row0:
            ref[row0:row1, :] = jnp.zeros((row1 - row0, ref.shape[1]), dtype)

    for ref, dtype in ((qt, BF), (vt, BF), (numt, F32), (wo, BF)):
        clear(ref, 0, koff, dtype)
        clear(ref, koff + inner, kw, dtype)

    for j in (0, kw // BLK - 1):
        dent[j] = jnp.zeros((8, toks), F32)

    for copy in smalls[:2]:
        copy.wait()
    span_row = span_ref[...].astype(F32)
    span_col = jnp.transpose(jnp.broadcast_to(span_row, (LANE, toks)))[:, 0:1]
    first_seg = span_row[:, 0:1]
    last_seg = span_row[:, toks - 1 : toks]
    lasts = [span_row[:, (c + 1) * chunk - 1 : (c + 1) * chunk] for c in range(2)]
    for c in range(2):
        rs = slice(c * chunk, (c + 1) * chunk)
        sr = span_row[:, rs]
        keep[c] = ((span_col[rs, :] <= sr) & (sr < lasts[c])).astype(F32).astype(BF)
    vwt[...] = jnp.transpose(vw[...])

    def turn(i, c):
        cols = pl.ds(pl.multiple_of(i * LANE, LANE), LANE)
        hcopy(i).wait()
        hid[cols, :] = jnp.transpose(hidt[:, cols])
        return c

    lax.fori_loop(0, toks // LANE, turn, 0)
    fetch(2)

    if rest:
        wcopy(full).wait()
        tail_w = jnp.transpose(wq[:, full * BLK : total])
        row = full * BLK - 2 * inner + koff
        vt[row : row + rest, :] = dot(tail_w, hidt[...]).astype(BF)

    def finish(out, b, rs):
        begin, end = b * BLK, b * BLK + BLK
        if begin < 2 * inner:
            pos = jnp.maximum(out, jnp.zeros_like(out))
            if end > 2 * inner:
                pos = jnp.where(iota(out.shape, 1) < 2 * inner - begin, pos, out)
            out = pos
        if end > inner and begin < 2 * inner:
            kp[rs, begin - lo * BLK : end - lo * BLK] = out
        if begin < inner:
            rows = min(end, inner) - begin
            qt[koff + begin : koff + begin + rows, rs] = jnp.transpose(out)[:rows]
        if end > 2 * inner:
            skip = max(2 * inner - begin, 0)
            row = begin + skip - 2 * inner + koff
            vt[row : row + BLK - skip, rs] = jnp.transpose(out)[skip:]

    def project(blocks):
        for b in blocks:
            wcopy(b).wait()
        fetch(3)
        for at, b in enumerate(blocks):
            cols = slice(b * BLK, b * BLK + BLK)
            pair = len(blocks) % 2 == 1 and at == len(blocks) - 1
            for rs in [slice(0, chunk), slice(chunk, toks)] if pair else [slice(0, toks)]:
                finish(dot(hid[rs, :], wq[:, cols]).astype(BF), b, rs)

    early = list(range(lo, full))
    for at in range(0, len(early) - 1, 2):
        project(early[at : at + (2 if at + 3 < len(early) else 3)])
    for copy in smalls[2:]:
        copy.wait()

    ones16 = jnp.ones((16, chunk), F32).astype(BF)
    lead_row = (span_row == first_seg).astype(F32).astype(BF)
    b0_row = (span_row[:, chunk:] <= lasts[0]).astype(F32).astype(BF)
    lane_slot = iota((HDIM, LANE), 1) // HDIM

    def diag(res, t):
        parts = [res[(t * PER + i) * HDIM : (t * PER + i + 1) * HDIM, t * LANE : (t + 1) * LANE] for i in range(PER)]
        out = parts[PER - 1]
        for i in range(PER - 2, -1, -1):
            out = jnp.where(lane_slot == i, parts[i], out)
        return out

    for j in range(tiles // 2):
        cols = slice(j * BLK, (j + 1) * BLK)
        res = []
        for c in range(2):
            rs = slice(c * chunk, (c + 1) * chunk)
            k8 = kp[rs, cols]
            lhs = jnp.concatenate([vt[cols, rs], ones16], axis=0)
            res.append(dot(lhs, k8))
            res.append(dot(lhs * lead_row[:, rs], k8))
            if c == 1:
                res.append(dot(lhs * b0_row, k8))
        c0, l0, c1, l1, b0 = res
        for t in range(2):
            u = 2 * j + t
            s0 = diag(c0, t)
            st_c0[u] = s0
            st_b0[u] = s0 + diag(b0, t)
            st_send[u] = (s0 + diag(c1, t)).astype(BF)
            lead_send[u] = (diag(l0, t) + diag(l1, t)).astype(BF)
            at = slice(t * LANE, (t + 1) * LANE)
            one = slice(BLK, BLK + 1)
            sum_c0[0, u : u + 1, :] = c0[one, at]
            sum_b0[0, u : u + 1, :] = c0[one, at] + b0[one, at]
            sum_c0[1, u : u + 1, :] = c0[one, at] + c1[one, at]
            sum_b0[1, u : u + 1, :] = l0[one, at] + l1[one, at]

    half = HDIM // 2
    row_no = iota((half, LANE), 0)

    def pack_sums(dst, sums):
        sums = jnp.where(row_no < tiles, sums, 0.0)
        high = sums.astype(BF).astype(F32)
        low = sums - high
        high = jnp.where(row_no == half - 1, jnp.broadcast_to(first_seg, (half, LANE)), high)
        dst[tiles] = jnp.concatenate([high, low], axis=0).astype(BF)
        for u in range(tiles + 1, units):
            dst[u] = jnp.zeros((HDIM, LANE), F32).astype(BF)

    pack_sums(st_send, sum_c0[1])
    pack_sums(lead_send, sum_b0[1])

    pl.semaphore_wait(barrier, n - 1)

    def part_copy(k):
        to = lax.rem(mate + k, TEAM)
        return remote(
            st_send.at[pl.ds(part * to, part)], part_recv.at[mate],
            psend.at[k], precv.at[mate], team * TEAM + to,
        )

    for k in range(1, TEAM):
        part_copy(k).start()

    def lead_copy(k):
        return remote(
            lead_send, lead_recv.at[k], lead_ssem.at[k], lead_rsem.at[k],
            lax.rem(me - 1 - k + n, n),
        )

    for k in range(2):

        @pl.when(me >= k + 1)
        def _(k=k):
            lead_copy(k).start()

    mine = map_ref[:, pl.ds(pl.multiple_of(me * toks, toks), toks)]
    target = mine // toks
    within = mine - target * toks
    hits = (iota((n, toks), 0) == jnp.broadcast_to(target, (n, toks))).astype(F32)
    upper = (iota((toks, toks), 0) <= iota((toks, toks), 1)).astype(BF)
    cum = dot(hits.astype(BF), upper)
    rank = jnp.sum(cum * hits, axis=0, keepdims=True).astype(jnp.int32) - 1
    slot = target * share + rank
    onehot[...] = (iota((toks, toks), 0) == jnp.broadcast_to(slot, (toks, toks))).astype(F32).astype(BF)
    line = (within // IW).astype(F32)
    spot = (within - within // IW * IW).astype(F32)
    row_at = iota((128, toks), 0)
    places = jnp.where(row_at == HDIM, jnp.broadcast_to(spot, (128, toks)), 0.0)
    places = jnp.where(row_at == HDIM + 1, jnp.broadcast_to(line, (128, toks)), places)
    xlat[...] = places

    part_recv[mate] = st_send[pl.ds(part * mate, part)]
    for k in range(1, TEAM):
        src = lax.rem(mate + k, TEAM)
        remote(
            st_send.at[pl.ds(0, part)], part_recv.at[src], psend.at[k], precv.at[src], team * TEAM + src
        ).wait_recv()
    whole = part_recv[0].astype(F32)
    for src in range(1, TEAM):
        whole = whole + part_recv[src].astype(F32)
    plane_send[...] = whole.astype(BF)

    def plane_copy(to):
        return remote(
            plane_send, plane_recv.at[team], gsend.at[to], grecv.at[team], TEAM * to + mate
        )

    for to in range(1, teams):

        @pl.when(team < to)
        def _(to=to):
            plane_copy(to).start()

    fetch(len(pending))
    project(list(range(lo)))

    def attend(jobs):
        def place(j, s):
            t, i = s // PER, s % PER
            if isinstance(j, int):
                return pl.ds(j * BLK + s * HDIM, HDIM), pl.ds(j * BLK + t * LANE, LANE), i
            return (
                pl.ds(pl.multiple_of(j * BLK + s * HDIM, HDIM), HDIM),
                pl.ds(pl.multiple_of(j * BLK + t * LANE, LANE), LANE), i,
            )

        def scores(j, s, c):
            rs = slice(c * chunk, (c + 1) * chunk)
            head, tile, i = place(j, s)
            pieces = [qt[head, rs]]
            if i:
                pieces = [jnp.zeros((i * HDIM, chunk), BF)] + pieces
            if i < PER - 1:
                pieces = pieces + [jnp.zeros(((PER - 1 - i) * HDIM, chunk), BF)]
            return dot(kp[rs, tile], jnp.concatenate(pieces, axis=0)).astype(BF) * keep[c]

        def values(j, s, c, score):
            rs = slice(c * chunk, (c + 1) * chunk)
            head, _, _ = place(j, s)
            out = dot(jnp.concatenate([vt[head, rs], ones16], axis=0), score)
            numt[head, rs] = out[:HDIM]
            dent[j, s : s + 1, rs] = out[HDIM : HDIM + 1]

        queue = []
        for job in jobs:
            queue.append((job, scores(*job)))
            if len(queue) > LAG:
                old, score = queue.pop(0)
                values(*old, score)
        for old, score in queue:
            values(*old, score)

    slots_of = BLK // HDIM
    groups = kw // BLK
    plain, extra = [], []
    for j in range(groups):
        slots = [s for s in range(slots_of) if first_slot <= j * slots_of + s < last_slot]
        if len(slots) == slots_of:
            plain.append(j)
        else:
            extra += [(j, s, c) for s in slots for c in range(2)]
    attend(extra)

    def attend_loop(j, carry_in):
        attend([(j, s, c) for s in range(slots_of) for c in range(2)])
        return carry_in

    lax.fori_loop(plain[0], plain[-1] + 1, attend_loop, 0)

    base[...] = jnp.zeros_like(base)
    for src in range(teams - 1):

        @pl.when(src < team)
        def _(src=src):
            remote(
                plane_send, plane_recv.at[src], gsend.at[src], grecv.at[src], TEAM * src + mate
            ).wait_recv()
            base[...] = base[...] + plane_recv[src].astype(F32)

    run = base[...]
    for m in range(TEAM):
        fin_send[m] = run.astype(BF)
        if m < TEAM - 1:
            run = run + part_recv[m].astype(F32)

    def fin_copy(k):
        to = lax.rem(mate + k, TEAM)
        return remote(
            fin_send.at[to], fin_recv.at[mate], fsend.at[k], frecv.at[mate], team * TEAM + to
        )

    for k in range(1, TEAM):
        fin_copy(k).start()

    after[...] = jnp.zeros_like(after)
    for k in range(2):

        @pl.when(me + 1 + k < n)
        def _(k=k):
            remote(
                lead_send, lead_recv.at[k], lead_ssem.at[k], lead_rsem.at[k], lax.rem(me + 1 + k, n)
            ).wait_recv()
            same = (lead_recv[k, tiles, half - 1 : half, 0:1].astype(F32) == last_seg).astype(F32)
            after[...] = after[...] + lead_recv[k].astype(F32) * same

    fin_recv[mate] = fin_send[mate]
    for k in range(1, TEAM):
        src = lax.rem(mate + k, TEAM)
        remote(
            fin_send.at[0], fin_recv.at[src], fsend.at[k], frecv.at[src], team * TEAM + src
        ).wait_recv()
    for m in range(TEAM):
        carry[m * part : (m + 1) * part] = fin_recv[m].astype(F32)

    reach = [(lasts[c] == last_seg).astype(F32) for c in range(2)]
    tails = [span_row[:, c * chunk : (c + 1) * chunk] == lasts[c] for c in range(2)]
    masks = [(lane_slot == i).astype(F32).astype(BF) for i in range(PER)]
    den_slot = iota((half, LANE), 0)
    den_lane = iota((half, LANE), 1) // HDIM
    den_live = lax.rem(den_slot, PER) == den_lane

    def sums_of(ref, u):
        return ref[tiles, pl.ds(u, 1), :] + ref[tiles, pl.ds(half + u, 1), :]

    def combine(j, carry_in):
        packs = [[], []]
        for t in range(2):
            u = 2 * j + t
            tile = pl.ds(pl.multiple_of(j * BLK + t * LANE, LANE), LANE)
            car, aft = carry[u], after[u]
            csum, asum = sums_of(carry, u), sums_of(after, u)
            for c in range(2):
                rs = slice(c * chunk, (c + 1) * chunk)
                if c == 0:
                    a_state, a_sum = car, csum
                    b_state = st_b0[u] + car + aft * reach[0]
                    b_sum = sum_b0[0, pl.ds(u, 1), :] + csum + asum * reach[0]
                else:
                    a_state, a_sum = st_c0[u] + car, sum_c0[0, pl.ds(u, 1), :] + csum
                    b_state = st_send[u].astype(F32) + car + aft
                    b_sum = sum_c0[1, pl.ds(u, 1), :] + csum + asum
                a16, b16 = a_state.astype(BF), b_state.astype(BF)
                dens = []
                for s in (a_sum, b_sum):
                    high = s.astype(BF).astype(F32)
                    dens.append((high, s - high))
                (ah, al), (bh, bl) = dens
                den = jnp.where(den_slot < PER, ah, jnp.where(den_slot < 2 * PER, al, jnp.where(den_slot < 3 * PER, bh, bl)))
                den = jnp.where(den_live, den, 0.0).astype(BF)
                lhs = jnp.concatenate([a16 * m for m in masks] + [b16 * m for m in masks] + [den], axis=0)
                res = dot(lhs, qt[tile, rs])
                tail = jnp.broadcast_to(tails[c], (LANE, chunk))
                numer = numt[tile, rs] + jnp.where(tail, res[LANE : 2 * LANE], res[:LANE])
                d_all = res[2 * LANE :]
                d_a = d_all[0:PER] + d_all[PER : 2 * PER]
                d_b = d_all[2 * PER : 3 * PER] + d_all[3 * PER :]
                d_loc = dent[j, t * PER : (t + 1) * PER, rs]
                inv = 1.0 / (1.0 + d_loc + jnp.where(tail[:PER], d_b, d_a))
                scaled = [numer[i * HDIM : (i + 1) * HDIM] * inv[i : i + 1] for i in range(PER)]
                packs[c].append(jnp.concatenate(scaled, axis=0).astype(BF))
        cols = pl.ds(pl.multiple_of(j * BLK, BLK), BLK)
        for c in range(2):
            att[c * chunk : (c + 1) * chunk, cols] = jnp.transpose(jnp.concatenate(packs[c], axis=0))
        return carry_in

    lax.fori_loop(0, groups, combine, 0)

    ocopy.wait()
    square = jnp.zeros((toks, LANE), F32)

    def rise(b):
        end = min(b + BLK, d)
        if d - b > BLK:
            return dot(att[...], wo[:, b:end])
        return jnp.concatenate([dot(att[:chunk, :], wo[:, b:end]), dot(att[chunk:, :], wo[:, b:end])], axis=0)

    def settle(b, part_sum, square):
        end = min(b + BLK, d)
        mixed = hid[:, b:end].astype(F32) + part_sum
        sq = mixed * mixed
        for x in range(0, end - b, LANE):
            width = min(LANE, end - b - x)
            piece = sq[:, x : x + width]
            if width < LANE:
                piece = jnp.concatenate([piece, jnp.zeros((toks, LANE - width), F32)], axis=1)
            square = square + piece
        ybuf[:, b:end] = (mixed * jnp.broadcast_to(gain[b:end][None, :], mixed.shape)).astype(BF)
        return square

    for b in range(0, d, BLK):
        square = settle(b, rise(b), square)
    vel[...] = dot(ybuf[...], vwt[...])
    meansq = jnp.sum(square, axis=1, keepdims=True) * (1.0 / d)
    step = vel[...] * (0.5 * lax.rsqrt(meansq + 1e-06))
    lat = noisy[...] - jnp.transpose(step)
    lat_out[...] = lat
    xlat[0:HDIM, :] = lat

    outgoing[...] = dot_nt(onehot[...], xlat[...].astype(BF)).astype(BF)

    def out_copy(k):
        to = lax.rem(me + k, n)
        return remote(
            outgoing.at[pl.ds(pl.multiple_of(to * share, share), share)],
            incoming.at[pl.ds(pl.multiple_of(me * share, share), share)],
            asend.at[k], arecv.at[me], to,
        )

    for k in range(1, n):
        out_copy(k).start()
    own = pl.ds(pl.multiple_of(me * share, share), share)
    incoming[own, :] = outgoing[own, :]
    for k in range(1, n):
        src = lax.rem(me + k, n)
        remote(
            outgoing.at[pl.ds(0, share)],
            incoming.at[pl.ds(pl.multiple_of(src * share, share), share)],
            asend.at[k], arecv.at[src], src,
        ).wait_recv()

    got = incoming[...]
    lane_no = iota((8, 128), 1)
    pick = jnp.where(lane_no == HDIM, 1.0, jnp.where(lane_no == HDIM + 1, float(IW), 0.0)).astype(BF)
    pos = dot_nt(pick, got)[0:1, :].astype(jnp.int32)
    onehot[...] = (iota((toks, toks), 0) == jnp.broadcast_to(pos, (toks, toks))).astype(F32).astype(BF)
    tile = dot(onehot[...], got)
    edge = 2 * IW
    wide[edge : edge + toks, :] = tile
    halo_send[0] = tile[:edge].astype(BF)
    halo_send[1] = tile[toks - edge :].astype(BF)

    def halo(k, to):
        return remote(halo_send.at[k], halo_recv.at[k], halo_ssem.at[k], halo_rsem.at[k], to)

    @pl.when(me > 0)
    def _():
        halo(0, me - 1).start()

    @pl.when(me < n - 1)
    def _():
        halo(1, me + 1).start()

    wide[0:edge, :] = jnp.zeros((edge, 128), F32)
    wide[edge + toks :, :] = jnp.zeros((edge, 128), F32)

    @pl.when(me > 0)
    def _():
        halo(1, me - 1).wait_recv()
        wide[0:edge, :] = halo_recv[1].astype(F32)

    @pl.when(me < n - 1)
    def _():
        halo(0, me + 1).wait_recv()
        wide[edge + toks :, :] = halo_recv[0].astype(F32)

    ext = toks + 2 * edge
    x = wide[...]
    column = lax.rem(iota((ext, 128), 0), IW)
    lane = iota((ext, 128), 1)
    left = jnp.where(column == 0, 0.0, pltpu.roll(x, 1, 0))
    right = jnp.where(column == IW - 1, 0.0, pltpu.roll(x, ext - 1, 0))
    three = jnp.where(
        lane < HDIM, left,
        jnp.where(lane < 2 * HDIM, pltpu.roll(x, HDIM, 1),
                  jnp.where(lane < 3 * HDIM, pltpu.roll(right, 2 * HDIM, 1), 0.0)),
    )
    three = three.astype(BF)
    mid = toks + 2 * IW
    k3 = 3 * HDIM
    acc = dot(three[0:mid, :k3], w1[0])
    acc = acc + dot(three[IW : IW + mid, :k3], w1[1])
    acc = acc + dot(three[2 * IW : 2 * IW + mid, :k3], w1[2])
    feat = acc / (1.0 + jnp.exp(-acc))
    row_at = iota((mid, 1), 0) // IW
    outside = ((row_at == 0) & (me == 0)) | ((row_at == mid // IW - 1) & (me == n - 1))
    feat = jnp.where(outside, 0.0, feat).astype(BF).astype(F32)
    column = lax.rem(iota((mid, 1), 0), IW)
    shifted[1] = feat.astype(BF)
    shifted[0] = jnp.where(column == 0, 0.0, pltpu.roll(feat, 1, 0)).astype(BF)
    shifted[2] = jnp.where(column == IW - 1, 0.0, pltpu.roll(feat, mid - 1, 0)).astype(BF)
    w2copy.wait()
    out = None
    for a in range(3):
        for b in range(3):
            piece = dot(shifted[b, a * IW : a * IW + toks, :], w2[3 * a + b])
            out = piece if out is None else out + piece
    dec_out[...] = out.astype(BF)

    for k in range(1, TEAM):
        part_copy(k).wait_send()
        fin_copy(k).wait_send()

    for k in range(2):

        @pl.when(me >= k + 1)
        def _(k=k):
            lead_copy(k).wait_send()

    for to in range(1, teams):

        @pl.when(team < to)
        def _(to=to):
            plane_copy(to).wait_send()

    for k in range(1, n):
        out_copy(k).wait_send()

    @pl.when(me > 0)
    def _():
        halo(0, me - 1).wait_send()

    @pl.when(me < n - 1)
    def _():
        halo(1, me + 1).wait_send()


def body(
    hidden_in, noisy_latents, span_ids, tile_map, qkv_weight, out_weight,
    norm_gain, velocity_weight, conv_first, conv_second,
):
    toks, d = hidden_in.shape
    inner = out_weight.shape[0]
    n = lax.axis_size("span")
    ch = conv_first.shape[3]
    chunk = toks // 2
    lo = inner // BLK
    koff = inner - lo * BLK
    kw = -(-(koff + inner) // BLK) * BLK
    tiles = kw // LANE
    units = -(-(tiles + 1) // TEAM) * TEAM
    part = units // TEAM
    teams = n // TEAM
    edge = 2 * IW
    mid = toks + 2 * IW
    blocks = -(-qkv_weight.shape[1] // BLK)
    vm, dma = pltpu.VMEM, pltpu.SemaphoreType.DMA
    any_, vmem = pl.BlockSpec(memory_space=pl.ANY), pl.BlockSpec(memory_space=pltpu.VMEM)
    maps = tile_map.shape[0]
    half = HDIM // 2
    scratch = [
        vm((HDIM, toks), F32), vm((1, toks), jnp.int32), vm((1, maps), jnp.int32),
        vm((d,), F32), vm((HDIM, d), BF), vm((3, 3 * HDIM, ch), BF),
        vm((d, toks), BF), vm((toks, d), BF), vm(qkv_weight.shape, BF), vm((kw, d), BF),
        vm((9, ch, ch), BF),
        vm((kw, toks), BF), vm((toks, kw), BF), vm((kw, toks), BF),
        vm((kw, toks), F32), vm((kw // BLK, 8, toks), F32), vm((2, chunk, chunk), BF),
        vm((toks, kw), BF), vm((toks, d), BF), vm((d, HDIM), BF), vm((toks, HDIM), F32),
        vm((tiles, HDIM, LANE), F32), vm((tiles, HDIM, LANE), F32),
        vm((2, half, LANE), F32), vm((2, half, LANE), F32),
        vm((units, HDIM, LANE), BF), vm((units, HDIM, LANE), BF), vm((2, units, HDIM, LANE), BF),
        vm((TEAM, part, HDIM, LANE), BF), vm((part, HDIM, LANE), BF), vm((teams, part, HDIM, LANE), BF),
        vm((TEAM, part, HDIM, LANE), BF), vm((TEAM, part, HDIM, LANE), BF),
        vm((part, HDIM, LANE), F32), vm((units, HDIM, LANE), F32), vm((units, HDIM, LANE), F32),
        vm((toks, toks), BF), vm((128, toks), F32),
        vm((toks, 128), BF), vm((toks, 128), BF),
        vm((toks + 2 * edge, 128), F32), vm((2, edge, 128), BF), vm((2, edge, 128), BF),
        vm((3, mid, ch), BF),
        dma((blocks,)), dma((3,)), dma((toks // LANE,)), dma((6,)), dma((TEAM,)), dma((TEAM,)), dma((teams,)), dma((teams,)),
        dma((TEAM,)), dma((TEAM,)),
        dma((2,)), dma((2,)), dma((n,)), dma((n,)), dma((2,)), dma((2,)),
    ]
    latents, decoded = pl.pallas_call(
        functools.partial(kernel, (n, toks, d, inner)),
        out_shape=(
            jax.ShapeDtypeStruct(noisy_latents.shape[::-1], F32),
            jax.ShapeDtypeStruct((toks, ch), BF),
        ),
        in_specs=[any_] * 10,
        out_specs=(vmem, vmem),
        scratch_shapes=scratch,
        compiler_params=pltpu.CompilerParams(
            collective_id=0, has_side_effects=True, vmem_limit_bytes=60 * 1024 * 1024
        ),
    )(
        hidden_in.T, noisy_latents.T, span_ids.reshape(1, toks), tile_map.reshape(1, -1),
        qkv_weight, out_weight, norm_gain, velocity_weight.T,
        conv_first.reshape(3, 3 * HDIM, ch), conv_second.reshape(9, ch, ch),
    )
    return latents.T, decoded.reshape(toks // IW, IW, ch)


def solution(mesh):
    rows = P(("groups", "span"), None)
    placed = (rows, rows, P(("groups", "span")), P("groups")) + (P(),) * 6
    return jax.shard_map(
        body, mesh=mesh, in_specs=placed,
        out_specs=(rows, P(("groups", "span"), None, None)), check_vma=False,
    )
```

```python
import functools

import jax
import jax.numpy as jnp
from jax import lax
from jax.experimental import pallas as pl
from jax.experimental.pallas import tpu as pltpu
from jax.sharding import PartitionSpec as P

HDIM = 32
IW = 64
BLK = 256
LANE = 128
PER = LANE // HDIM
TEAM = 4
LAG = 3
AHEAD = 4
BF = jnp.bfloat16
F32 = jnp.float32


def dot(a, b):
    return jnp.dot(a, b, preferred_element_type=F32)


def dot_nt(a, b):
    return lax.dot_general(a, b, (((1,), (1,)), ((), ())), preferred_element_type=F32)


def iota(shape, axis):
    return lax.broadcasted_iota(jnp.int32, shape, axis)


def kernel(
    cfg,
    hid_hbm, noisy_hbm, span_hbm, map_hbm, wq_hbm, wo_hbm, gain_hbm, vw_hbm, w1_hbm, w2_hbm,
    lat_out, dec_out,
    noisy, span_ref, map_ref, gain, vw, w1,
    hidt, hid, wq, wo, w2, qt, kp, vt, numt, dent, keep, att, ybuf, vwt,
    st_c0, st_b0, sum_c0, sum_b0, st_send, lead_send, lead_recv,
    part_recv, plane_send, plane_recv, fin_send, fin_recv, base, carry, after, onehot, map_rows, place, noisy_t, outgoing, incoming,
    wide, shifted,
    wsem, lsem, hsem, isem, psend, precv, gsend, grecv, fsend, frecv, lead_ssem, lead_rsem, asend, arecv,
):
    n, toks, d, inner = cfg
    me = lax.axis_index("span")
    mate = lax.rem(me, TEAM)
    team = me // TEAM
    teams = n // TEAM
    share = toks // n
    rows_to = share // PER
    chunk = toks // 2
    lo = inner // BLK
    koff = inner - lo * BLK
    kw = kp.shape[1]
    tiles = kw // LANE
    units = st_send.shape[0]
    part = units // TEAM
    heads = inner // HDIM
    first_slot = koff // HDIM
    last_slot = first_slot + heads

    def remote(src, dst, ss, rs, dev):
        return pltpu.make_async_remote_copy(
            src_ref=src, dst_ref=dst, send_sem=ss, recv_sem=rs,
            device_id={"span": dev}, device_id_type=pl.DeviceIdType.MESH,
        )

    total = wq_hbm.shape[1]
    full = total // BLK
    rest = total - full * BLK

    def wcopy(b):
        cols = slice(b * BLK, min(b * BLK + BLK, total))
        return pltpu.make_async_copy(wq_hbm.at[:, cols], wq.at[:, cols], wsem.at[b])

    def hcopy(i):
        cols = pl.ds(i * LANE if isinstance(i, int) else pl.multiple_of(i * LANE, LANE), LANE)
        return pltpu.make_async_copy(hid_hbm.at[:, cols], hidt.at[:, cols], hsem.at[i])

    for i in range(toks // LANE):
        hcopy(i).start()
    smalls = [
        pltpu.make_async_copy(src, dst, isem.at[i])
        for i, (src, dst) in enumerate([
            (span_hbm, span_ref), (vw_hbm, vw), (map_hbm, map_ref), (noisy_hbm, noisy),
            (gain_hbm, gain), (w1_hbm, w1),
        ])
    ]
    for copy in smalls[:2]:
        copy.start()
    ocopy = pltpu.make_async_copy(wo_hbm, wo.at[koff : koff + inner], lsem.at[1])
    w2copy = pltpu.make_async_copy(w2_hbm, w2, lsem.at[2])
    pending = [wcopy(full)] if rest else []
    pending += [wcopy(b) for b in range(lo, full)] + smalls[2:] + [wcopy(b) for b in range(lo)] + [ocopy, w2copy]

    def fetch(count):
        for copy in pending[:count]:
            copy.start()
        del pending[:count]

    fetch(AHEAD)

    barrier = pltpu.get_barrier_semaphore()
    for k in range(1, n):
        pl.semaphore_signal(
            barrier, inc=1, device_id={"span": lax.rem(me + k, n)},
            device_id_type=pl.DeviceIdType.MESH,
        )

    def clear(ref, row0, row1, dtype):
        if row1 > row0:
            ref[row0:row1, :] = jnp.zeros((row1 - row0, ref.shape[1]), dtype)

    for ref, dtype in ((qt, BF), (vt, BF), (numt, F32), (wo, BF)):
        clear(ref, 0, koff, dtype)
        clear(ref, koff + inner, kw, dtype)

    for j in (0, kw // BLK - 1):
        dent[j] = jnp.zeros((8, toks), F32)

    for copy in smalls[:2]:
        copy.wait()
    span_row = span_ref[...].astype(F32)
    span_col = jnp.transpose(jnp.broadcast_to(span_row, (LANE, toks)))[:, 0:1]
    first_seg = span_row[:, 0:1]
    last_seg = span_row[:, toks - 1 : toks]
    lasts = [span_row[:, (c + 1) * chunk - 1 : (c + 1) * chunk] for c in range(2)]
    for c in range(2):
        rs = slice(c * chunk, (c + 1) * chunk)
        sr = span_row[:, rs]
        keep[c] = ((span_col[rs, :] <= sr) & (sr < lasts[c])).astype(F32).astype(BF)
    vwt[...] = jnp.concatenate([jnp.transpose(vw[...]), jnp.zeros((d, LANE - HDIM), F32).astype(BF)], axis=1)

    def turn(i, c):
        cols = pl.ds(pl.multiple_of(i * LANE, LANE), LANE)
        hcopy(i).wait()
        hid[cols, :] = jnp.transpose(hidt[:, cols])
        return c

    lax.fori_loop(0, toks // LANE, turn, 0)
    fetch(2)

    if rest:
        wcopy(full).wait()
        tail_w = jnp.transpose(wq[:, full * BLK : total])
        row = full * BLK - 2 * inner + koff
        vt[row : row + rest, :] = dot(tail_w, hidt[...]).astype(BF)

    def finish(out, b, rs):
        begin, end = b * BLK, b * BLK + BLK
        if begin < 2 * inner:
            pos = jnp.maximum(out, jnp.zeros_like(out))
            if end > 2 * inner:
                pos = jnp.where(iota(out.shape, 1) < 2 * inner - begin, pos, out)
            out = pos
        if end > inner and begin < 2 * inner:
            kp[rs, begin - lo * BLK : end - lo * BLK] = out
        if begin < inner:
            rows = min(end, inner) - begin
            qt[koff + begin : koff + begin + rows, rs] = jnp.transpose(out)[:rows]
        if end > 2 * inner:
            skip = max(2 * inner - begin, 0)
            row = begin + skip - 2 * inner + koff
            vt[row : row + BLK - skip, rs] = jnp.transpose(out)[skip:]

    def project(blocks):
        for b in blocks:
            wcopy(b).wait()
        fetch(3)
        for at, b in enumerate(blocks):
            cols = slice(b * BLK, b * BLK + BLK)
            pair = len(blocks) % 2 == 1 and at == len(blocks) - 1
            for rs in [slice(0, chunk), slice(chunk, toks)] if pair else [slice(0, toks)]:
                finish(dot(hid[rs, :], wq[:, cols]).astype(BF), b, rs)

    early = list(range(lo, full))
    for at in range(0, len(early) - 1, 2):
        project(early[at : at + (2 if at + 3 < len(early) else 3)])
    for copy in smalls[2:]:
        copy.wait()

    ones16 = jnp.ones((16, chunk), F32).astype(BF)
    lead_row = (span_row == first_seg).astype(F32).astype(BF)
    b0_row = (span_row[:, chunk:] <= lasts[0]).astype(F32).astype(BF)
    lane_slot = iota((HDIM, LANE), 1) // HDIM

    def diag(res, t):
        parts = [res[(t * PER + i) * HDIM : (t * PER + i + 1) * HDIM, t * LANE : (t + 1) * LANE] for i in range(PER)]
        out = parts[PER - 1]
        for i in range(PER - 2, -1, -1):
            out = jnp.where(lane_slot == i, parts[i], out)
        return out

    for j in range(tiles // 2):
        cols = slice(j * BLK, (j + 1) * BLK)
        res = []
        for c in range(2):
            rs = slice(c * chunk, (c + 1) * chunk)
            k8 = kp[rs, cols]
            lhs = jnp.concatenate([vt[cols, rs], ones16], axis=0)
            res.append(dot(lhs, k8))
            res.append(dot(lhs * lead_row[:, rs], k8))
            if c == 1:
                res.append(dot(lhs * b0_row, k8))
        c0, l0, c1, l1, b0 = res
        for t in range(2):
            u = 2 * j + t
            s0 = diag(c0, t)
            st_c0[u] = s0
            st_b0[u] = s0 + diag(b0, t)
            st_send[u] = (s0 + diag(c1, t)).astype(BF)
            lead_send[u] = (diag(l0, t) + diag(l1, t)).astype(BF)
            at = slice(t * LANE, (t + 1) * LANE)
            one = slice(BLK, BLK + 1)
            sum_c0[0, u : u + 1, :] = c0[one, at]
            sum_b0[0, u : u + 1, :] = c0[one, at] + b0[one, at]
            sum_c0[1, u : u + 1, :] = c0[one, at] + c1[one, at]
            sum_b0[1, u : u + 1, :] = l0[one, at] + l1[one, at]

    half = HDIM // 2
    row_no = iota((half, LANE), 0)

    def pack_sums(dst, sums):
        sums = jnp.where(row_no < tiles, sums, 0.0)
        high = sums.astype(BF).astype(F32)
        low = sums - high
        high = jnp.where(row_no == half - 1, jnp.broadcast_to(first_seg, (half, LANE)), high)
        dst[tiles] = jnp.concatenate([high, low], axis=0).astype(BF)
        for u in range(tiles + 1, units):
            dst[u] = jnp.zeros((HDIM, LANE), F32).astype(BF)

    pack_sums(st_send, sum_c0[1])
    pack_sums(lead_send, sum_b0[1])

    pl.semaphore_wait(barrier, n - 1)

    def part_copy(k):
        to = lax.rem(mate + k, TEAM)
        return remote(
            st_send.at[pl.ds(part * to, part)], part_recv.at[mate],
            psend.at[k], precv.at[mate], team * TEAM + to,
        )

    for k in range(1, TEAM):
        part_copy(k).start()

    def lead_copy(k):
        return remote(
            lead_send, lead_recv.at[k], lead_ssem.at[k], lead_rsem.at[k],
            lax.rem(me - 1 - k + n, n),
        )

    mine = map_ref[:, pl.ds(pl.multiple_of(me * toks, toks), toks)]
    target = mine // toks
    for b in range(n):
        map_rows[b : b + 1, :] = map_ref[:, b * toks : (b + 1) * toks]
    goal = map_rows[...] // toks
    where_in = map_rows[...] - goal * toks
    hits = [iota((n, toks), 0) == jnp.broadcast_to(target, (n, toks))]
    hits += [goal == me - 1 + x for x in range(3)]
    upper = (iota((toks, toks), 0) <= iota((toks, toks), 1)).astype(BF)
    cum = dot(jnp.concatenate([h.astype(F32) for h in hits], axis=0).astype(BF), upper)
    rank = jnp.sum(jnp.where(hits[0], cum[:n], 0.0), axis=0, keepdims=True).astype(jnp.int32) - 1
    packed = n * rows_to
    slot = rank // rows_to * packed + target * rows_to + lax.rem(rank, rows_to)
    onehot[...] = (iota((toks, toks), 0) == jnp.broadcast_to(slot, (toks, toks))).astype(F32).astype(BF)
    spot_f = where_in.astype(F32)
    lane_n = iota((n, LANE), 1)
    found = []
    for x in range(3):
        order = jnp.where(hits[1 + x], cum[n * (1 + x) : n * (2 + x)], 0.0)
        table = jnp.zeros((n, LANE), F32)
        for r in range(share):
            one = jnp.sum(jnp.where(order == float(r + 1), spot_f, 0.0), axis=1, keepdims=True)
            table = jnp.where(lane_n == r, one, table)
        whole_pos = table.astype(jnp.int32)
        found.append((whole_pos // IW).astype(F32))
        found.append(lax.rem(whole_pos, IW).astype(F32))
    slot_no = iota((LANE, toks), 1)
    rank_of = slot_no // packed * rows_to + lax.rem(slot_no, rows_to)
    spread = (iota((LANE, toks), 0) == rank_of).astype(F32).astype(BF)
    filled = dot(jnp.concatenate(found, axis=0).astype(BF), spread)
    source = lax.rem(iota((n, toks), 1), packed) // rows_to
    owned = iota((n, toks), 0) == source
    edge = 2 * IW
    starts = (0, edge, edge + toks)
    sizes = (edge, toks, edge)
    for x in range(3):
        lines, spots = [
            jnp.sum(jnp.where(owned, filled[n * (2 * x + y) : n * (2 * x + y + 1)], 0.0), axis=0, keepdims=True)
            for y in range(2)
        ]
        pos = (lines * float(IW) + spots).astype(jnp.int32)
        if x == 0:
            pos = pos - (toks - edge)
        place[starts[x] : starts[x] + sizes[x], :] = (
            iota((sizes[x], toks), 0) == jnp.broadcast_to(pos, (sizes[x], toks))
        ).astype(F32).astype(BF)
    for x in (0, n + 1):
        outgoing[x] = jnp.zeros((rows_to, LANE), F32).astype(BF)
    noisy_t[...] = jnp.concatenate(
        [jnp.transpose(noisy[...]), jnp.zeros((toks, LANE - HDIM), F32)], axis=1
    )

    fetch(len(pending))
    project(list(range(lo // 2)))

    part_recv[mate] = st_send[pl.ds(part * mate, part)]
    for k in range(1, TEAM):
        src = lax.rem(mate + k, TEAM)
        remote(
            st_send.at[pl.ds(0, part)], part_recv.at[src], psend.at[k], precv.at[src], team * TEAM + src
        ).wait_recv()
    whole = part_recv[0].astype(F32)
    for src in range(1, TEAM):
        whole = whole + part_recv[src].astype(F32)
    plane_send[...] = whole.astype(BF)

    def plane_copy(to):
        return remote(
            plane_send, plane_recv.at[team], gsend.at[to], grecv.at[team], TEAM * to + mate
        )

    for to in range(teams - 1, 0, -1):

        @pl.when(team < to)
        def _(to=to):
            plane_copy(to).start()

    for k in range(2):

        @pl.when(me >= k + 1)
        def _(k=k):
            lead_copy(k).start()

    project(list(range(lo // 2, lo)))

    def attend(jobs):
        def place(j, s):
            t, i = s // PER, s % PER
            if isinstance(j, int):
                return pl.ds(j * BLK + s * HDIM, HDIM), pl.ds(j * BLK + t * LANE, LANE), i
            return (
                pl.ds(pl.multiple_of(j * BLK + s * HDIM, HDIM), HDIM),
                pl.ds(pl.multiple_of(j * BLK + t * LANE, LANE), LANE), i,
            )

        def scores(j, s, c):
            rs = slice(c * chunk, (c + 1) * chunk)
            head, tile, i = place(j, s)
            pieces = [qt[head, rs]]
            if i:
                pieces = [jnp.zeros((i * HDIM, chunk), BF)] + pieces
            if i < PER - 1:
                pieces = pieces + [jnp.zeros(((PER - 1 - i) * HDIM, chunk), BF)]
            return dot(kp[rs, tile], jnp.concatenate(pieces, axis=0)).astype(BF) * keep[c]

        def values(j, s, c, score):
            rs = slice(c * chunk, (c + 1) * chunk)
            head, _, _ = place(j, s)
            out = dot(jnp.concatenate([vt[head, rs], ones16], axis=0), score)
            numt[head, rs] = out[:HDIM]
            dent[j, s : s + 1, rs] = out[HDIM : HDIM + 1]

        queue = []
        for job in jobs:
            queue.append((job, scores(*job)))
            if len(queue) > LAG:
                old, score = queue.pop(0)
                values(*old, score)
        for old, score in queue:
            values(*old, score)

    slots_of = BLK // HDIM
    groups = kw // BLK
    plain, extra = [], []
    for j in range(groups):
        slots = [s for s in range(slots_of) if first_slot <= j * slots_of + s < last_slot]
        if len(slots) == slots_of:
            plain.append(j)
        else:
            extra += [(j, s, c) for s in slots for c in range(2)]
    attend(extra)

    def attend_loop(j, carry_in):
        attend([(j, s, c) for s in range(slots_of) for c in range(2)])
        return carry_in

    lax.fori_loop(plain[0], plain[-1], attend_loop, 0)

    base[...] = jnp.zeros_like(base)
    for src in range(teams - 1):

        @pl.when(src < team)
        def _(src=src):
            remote(
                plane_send, plane_recv.at[src], gsend.at[src], grecv.at[src], TEAM * src + mate
            ).wait_recv()
            base[...] = base[...] + plane_recv[src].astype(F32)

    run = base[...]
    for m in range(TEAM):
        fin_send[m] = run.astype(BF)
        if m < TEAM - 1:
            run = run + part_recv[m].astype(F32)

    def fin_copy(k):
        to = lax.rem(mate + k, TEAM)
        return remote(
            fin_send.at[to], fin_recv.at[mate], fsend.at[k], frecv.at[mate], team * TEAM + to
        )

    for k in range(1, TEAM):
        fin_copy(k).start()

    lax.fori_loop(plain[-1], plain[-1] + 1, attend_loop, 0)

    after[...] = jnp.zeros_like(after)
    for k in range(2):

        @pl.when(me + 1 + k < n)
        def _(k=k):
            remote(
                lead_send, lead_recv.at[k], lead_ssem.at[k], lead_rsem.at[k], lax.rem(me + 1 + k, n)
            ).wait_recv()
            same = (lead_recv[k, tiles, half - 1 : half, 0:1].astype(F32) == last_seg).astype(F32)
            after[...] = after[...] + lead_recv[k].astype(F32) * same

    fin_recv[mate] = fin_send[mate]
    for k in range(1, TEAM):
        src = lax.rem(mate + k, TEAM)
        remote(
            fin_send.at[0], fin_recv.at[src], fsend.at[k], frecv.at[src], team * TEAM + src
        ).wait_recv()
    for m in range(TEAM):
        carry[m * part : (m + 1) * part] = fin_recv[m].astype(F32)

    reach = [(lasts[c] == last_seg).astype(F32) for c in range(2)]
    tails = [span_row[:, c * chunk : (c + 1) * chunk] == lasts[c] for c in range(2)]
    masks = [(lane_slot == i).astype(F32).astype(BF) for i in range(PER)]
    den_slot = iota((half, LANE), 0)
    den_lane = iota((half, LANE), 1) // HDIM
    den_live = lax.rem(den_slot, PER) == den_lane

    def sums_of(ref, u):
        return ref[tiles, pl.ds(u, 1), :] + ref[tiles, pl.ds(half + u, 1), :]

    def combine(j, carry_in):
        packs = [[], []]
        for t in range(2):
            u = 2 * j + t
            tile = pl.ds(pl.multiple_of(j * BLK + t * LANE, LANE), LANE)
            car, aft = carry[u], after[u]
            csum, asum = sums_of(carry, u), sums_of(after, u)
            for c in range(2):
                rs = slice(c * chunk, (c + 1) * chunk)
                if c == 0:
                    a_state, a_sum = car, csum
                    b_state = st_b0[u] + car + aft * reach[0]
                    b_sum = sum_b0[0, pl.ds(u, 1), :] + csum + asum * reach[0]
                else:
                    a_state, a_sum = st_c0[u] + car, sum_c0[0, pl.ds(u, 1), :] + csum
                    b_state = st_send[u].astype(F32) + car + aft
                    b_sum = sum_c0[1, pl.ds(u, 1), :] + csum + asum
                a16, b16 = a_state.astype(BF), b_state.astype(BF)
                dens = []
                for s in (a_sum, b_sum):
                    high = s.astype(BF).astype(F32)
                    dens.append((high, s - high))
                (ah, al), (bh, bl) = dens
                den = jnp.where(den_slot < PER, ah, jnp.where(den_slot < 2 * PER, al, jnp.where(den_slot < 3 * PER, bh, bl)))
                den = jnp.where(den_live, den, 0.0).astype(BF)
                lhs = jnp.concatenate([a16 * m for m in masks] + [b16 * m for m in masks] + [den], axis=0)
                res = dot(lhs, qt[tile, rs])
                tail = jnp.broadcast_to(tails[c], (LANE, chunk))
                numer = numt[tile, rs] + jnp.where(tail, res[LANE : 2 * LANE], res[:LANE])
                d_all = res[2 * LANE :]
                d_a = d_all[0:PER] + d_all[PER : 2 * PER]
                d_b = d_all[2 * PER : 3 * PER] + d_all[3 * PER :]
                d_loc = dent[j, t * PER : (t + 1) * PER, rs]
                inv = 1.0 / (1.0 + d_loc + jnp.where(tail[:PER], d_b, d_a))
                scaled = [numer[i * HDIM : (i + 1) * HDIM] * inv[i : i + 1] for i in range(PER)]
                packs[c].append(jnp.concatenate(scaled, axis=0).astype(BF))
        cols = pl.ds(pl.multiple_of(j * BLK, BLK), BLK)
        for c in range(2):
            att[c * chunk : (c + 1) * chunk, cols] = jnp.transpose(jnp.concatenate(packs[c], axis=0))
        return carry_in

    lax.fori_loop(0, groups, combine, 0)

    ocopy.wait()
    square = jnp.zeros((toks, LANE), F32)

    def rise(b):
        end = min(b + BLK, d)
        if d - b > BLK:
            return dot(att[...], wo[:, b:end])
        return jnp.concatenate([dot(att[:chunk, :], wo[:, b:end]), dot(att[chunk:, :], wo[:, b:end])], axis=0)

    def settle(b, part_sum, square):
        end = min(b + BLK, d)
        mixed = hid[:, b:end].astype(F32) + part_sum
        sq = mixed * mixed
        for x in range(0, end - b, LANE):
            width = min(LANE, end - b - x)
            piece = sq[:, x : x + width]
            if width < LANE:
                piece = jnp.concatenate([piece, jnp.zeros((toks, LANE - width), F32)], axis=1)
            square = square + piece
        ybuf[:, b:end] = (mixed * jnp.broadcast_to(gain[b:end][None, :], mixed.shape)).astype(BF)
        return square

    for b in range(0, d, BLK):
        square = settle(b, rise(b), square)
    vel = dot(ybuf[...], vwt[...])
    meansq = jnp.sum(square, axis=1, keepdims=True) * (1.0 / d)
    lat = noisy_t[...] - vel * (0.5 * lax.rsqrt(meansq + 1e-06))
    noisy_t[...] = lat
    sorted_lat = dot(onehot[...], lat.astype(BF))
    dense = sorted_lat[:packed]
    for a in range(1, PER):
        dense = dense + pltpu.roll(sorted_lat[a * packed : (a + 1) * packed], a * HDIM, 1)
    outgoing[1 : n + 1] = dense.reshape(n, rows_to, LANE).astype(BF)

    def flip(k):
        to, bit = 0, 1
        while bit < n:
            have = lax.rem(me // bit, 2)
            to = to + bit * (1 - have if k & bit else have)
            bit *= 2
        return to

    def out_copy(k):
        to = flip(k)
        return remote(outgoing.at[pl.ds(to, 3)], incoming.at[me], asend.at[k], arecv.at[me], to)

    for k in range(n - 1, 0, -1):
        out_copy(k).start()
    incoming[me] = outgoing[pl.ds(me, 3)]
    lat_out[...] = jnp.transpose(noisy_t[...])[:HDIM]
    for k in range(1, n):
        src = flip(k)
        remote(outgoing.at[pl.ds(0, 3)], incoming.at[src], asend.at[k], arecv.at[src], src).wait_recv()

    for x in range(3):
        dense = incoming[:, x].astype(F32).reshape(packed, LANE)
        slots = [dense] + [pltpu.roll(dense, LANE - a * HDIM, 1) for a in range(1, PER)]
        at = slice(starts[x], starts[x] + sizes[x])
        wide[at, :] = dot(place[at, :], jnp.concatenate(slots, axis=0).astype(BF))

    ext = toks + 2 * edge
    x = wide[...]
    column = lax.rem(iota((ext, 128), 0), IW)
    lane = iota((ext, 128), 1)
    left = jnp.where(column == 0, 0.0, pltpu.roll(x, 1, 0))
    right = jnp.where(column == IW - 1, 0.0, pltpu.roll(x, ext - 1, 0))
    three = jnp.where(
        lane < HDIM, left,
        jnp.where(lane < 2 * HDIM, pltpu.roll(x, HDIM, 1),
                  jnp.where(lane < 3 * HDIM, pltpu.roll(right, 2 * HDIM, 1), 0.0)),
    )
    three = three.astype(BF)
    mid = toks + 2 * IW
    k3 = 3 * HDIM
    acc = dot(three[0:mid, :k3], w1[0])
    acc = acc + dot(three[IW : IW + mid, :k3], w1[1])
    acc = acc + dot(three[2 * IW : 2 * IW + mid, :k3], w1[2])
    feat = acc / (1.0 + jnp.exp(-acc))
    row_at = iota((mid, 1), 0) // IW
    outside = ((row_at == 0) & (me == 0)) | ((row_at == mid // IW - 1) & (me == n - 1))
    feat = jnp.where(outside, 0.0, feat).astype(BF).astype(F32)
    column = lax.rem(iota((mid, 1), 0), IW)
    shifted[1] = feat.astype(BF)
    shifted[0] = jnp.where(column == 0, 0.0, pltpu.roll(feat, 1, 0)).astype(BF)
    shifted[2] = jnp.where(column == IW - 1, 0.0, pltpu.roll(feat, mid - 1, 0)).astype(BF)
    w2copy.wait()
    out = None
    for a in range(3):
        for b in range(3):
            piece = dot(shifted[b, a * IW : a * IW + toks, :], w2[3 * a + b])
            out = piece if out is None else out + piece
    dec_out[...] = out.astype(BF)

    for k in range(1, TEAM):
        part_copy(k).wait_send()
        fin_copy(k).wait_send()

    for k in range(2):

        @pl.when(me >= k + 1)
        def _(k=k):
            lead_copy(k).wait_send()

    for to in range(1, teams):

        @pl.when(team < to)
        def _(to=to):
            plane_copy(to).wait_send()

    for k in range(1, n):
        out_copy(k).wait_send()


def flush(lat, dec, lat_out, dec_out, sem):
    copies = [
        pltpu.make_async_copy(dec, dec_out, sem.at[0]),
        pltpu.make_async_copy(lat, lat_out, sem.at[1]),
    ]
    for copy in copies:
        copy.start()
    for copy in copies:
        copy.wait()


def body(
    hidden_in, noisy_latents, span_ids, tile_map, qkv_weight, out_weight,
    norm_gain, velocity_weight, conv_first, conv_second,
):
    toks, d = hidden_in.shape
    inner = out_weight.shape[0]
    n = lax.axis_size("span")
    ch = conv_first.shape[3]
    chunk = toks // 2
    lo = inner // BLK
    koff = inner - lo * BLK
    kw = -(-(koff + inner) // BLK) * BLK
    tiles = kw // LANE
    units = -(-(tiles + 1) // TEAM) * TEAM
    part = units // TEAM
    teams = n // TEAM
    edge = 2 * IW
    mid = toks + 2 * IW
    blocks = -(-qkv_weight.shape[1] // BLK)
    vm, dma = pltpu.VMEM, pltpu.SemaphoreType.DMA
    any_, vmem = pl.BlockSpec(memory_space=pl.ANY), pl.BlockSpec(memory_space=pltpu.VMEM)
    maps = tile_map.shape[0]
    half = HDIM // 2
    rows_to = toks // n // PER
    scratch = [
        vm((HDIM, toks), F32), vm((1, toks), jnp.int32), vm((1, maps), jnp.int32),
        vm((d,), F32), vm((HDIM, d), BF), vm((3, 3 * HDIM, ch), BF),
        vm((d, toks), BF), vm((toks, d), BF), vm(qkv_weight.shape, BF), vm((kw, d), BF),
        vm((9, ch, ch), BF),
        vm((kw, toks), BF), vm((toks, kw), BF), vm((kw, toks), BF),
        vm((kw, toks), F32), vm((kw // BLK, 8, toks), F32), vm((2, chunk, chunk), BF),
        vm((toks, kw), BF), vm((toks, d), BF), vm((d, LANE), BF),
        vm((tiles, HDIM, LANE), F32), vm((tiles, HDIM, LANE), F32),
        vm((2, half, LANE), F32), vm((2, half, LANE), F32),
        vm((units, HDIM, LANE), BF), vm((units, HDIM, LANE), BF), vm((2, units, HDIM, LANE), BF),
        vm((TEAM, part, HDIM, LANE), BF), vm((part, HDIM, LANE), BF), vm((teams, part, HDIM, LANE), BF),
        vm((TEAM, part, HDIM, LANE), BF), vm((TEAM, part, HDIM, LANE), BF),
        vm((part, HDIM, LANE), F32), vm((units, HDIM, LANE), F32), vm((units, HDIM, LANE), F32),
        vm((toks, toks), BF), vm((n, toks), jnp.int32), vm((toks + 2 * edge, toks), BF), vm((toks, LANE), F32),
        vm((n + 2, rows_to, LANE), BF), vm((n, 3, rows_to, LANE), BF),
        vm((toks + 2 * edge, 128), F32),
        vm((3, mid, ch), BF),
        dma((blocks,)), dma((3,)), dma((toks // LANE,)), dma((6,)), dma((TEAM,)), dma((TEAM,)), dma((teams,)), dma((teams,)),
        dma((TEAM,)), dma((TEAM,)),
        dma((2,)), dma((2,)), dma((n,)), dma((n,)),
    ]
    latents, decoded = pl.pallas_call(
        functools.partial(kernel, (n, toks, d, inner)),
        out_shape=(
            pltpu.VMEM(noisy_latents.shape[::-1], F32),
            pltpu.VMEM((toks, ch), BF),
        ),
        in_specs=[any_] * 10,
        out_specs=(vmem, vmem),
        scratch_shapes=scratch,
        compiler_params=pltpu.CompilerParams(
            collective_id=0, has_side_effects=True, vmem_limit_bytes=60 * 1024 * 1024
        ),
    )(
        hidden_in.T, noisy_latents.T, span_ids.reshape(1, toks), tile_map.reshape(1, -1),
        qkv_weight, out_weight, norm_gain, velocity_weight.T,
        conv_first.reshape(3, 3 * HDIM, ch), conv_second.reshape(9, ch, ch),
    )
    latents, decoded = [pltpu.with_memory_space_constraint(x, pltpu.VMEM) for x in (latents, decoded)]
    latents, decoded = pl.pallas_call(
        flush,
        out_shape=(
            jax.ShapeDtypeStruct(latents.shape, F32),
            jax.ShapeDtypeStruct(decoded.shape, BF),
        ),
        in_specs=[vmem, vmem],
        out_specs=(any_, any_),
        scratch_shapes=[dma((2,))],
    )(latents, decoded)
    return latents.T, decoded.reshape(toks // IW, IW, ch)


def solution(mesh):
    rows = P(("groups", "span"), None)
    placed = (rows, rows, P(("groups", "span")), P("groups")) + (P(),) * 6
    return jax.shard_map(
        body, mesh=mesh, in_specs=placed,
        out_specs=(rows, P(("groups", "span"), None, None)), check_vma=False,
    )
```

```python
import functools

import jax
import jax.numpy as jnp
from jax import lax
from jax.experimental import pallas as pl
from jax.experimental.pallas import tpu as pltpu
from jax.sharding import PartitionSpec as P

HDIM = 32
IW = 64
BLK = 256
LANE = 128
PER = LANE // HDIM
TEAM = 4
LAG = 3
AHEAD = 4
BF = jnp.bfloat16
F32 = jnp.float32


def dot(a, b):
    return jnp.dot(a, b, preferred_element_type=F32)


def dot_nt(a, b):
    return lax.dot_general(a, b, (((1,), (1,)), ((), ())), preferred_element_type=F32)


def iota(shape, axis):
    return lax.broadcasted_iota(jnp.int32, shape, axis)


def kernel(
    cfg,
    hid_hbm, noisy_hbm, span_hbm, map_hbm, wq_hbm, wo_hbm, gain_hbm, vw_hbm, w1_hbm, w2_hbm,
    lat_out, dec_out,
    noisy, span_ref, map_ref, gain, vw, w1,
    hidt, hid, wq, wo, w2, qt, kp, vt, numt, dent, keep, att, ybuf, vwt,
    st_c0, st_b0, st_all, st_lead, sum_c0, sum_b0, st_send, lead_send, lead_recv,
    part_recv, plane_send, plane_recv, fin_send, fin_recv, base, carry, after, onehot, map_rows, place, noisy_t, outgoing, incoming,
    wide, shifted,
    wsem, lsem, hsem, isem, psend, precv, gsend, grecv, fsend, frecv, lead_ssem, lead_rsem, asend, arecv,
):
    n, toks, d, inner = cfg
    me = lax.axis_index("span")
    mate = lax.rem(me, TEAM)
    team = me // TEAM
    teams = n // TEAM
    share = toks // n
    rows_to = share // PER
    chunk = toks // 2
    lo = inner // BLK
    koff = inner - lo * BLK
    kw = kp.shape[1]
    tiles = kw // LANE
    units = st_send.shape[0] // 2
    part = 2 * units // TEAM
    half = HDIM // 2
    heads = inner // HDIM
    first_slot = koff // HDIM
    last_slot = first_slot + heads

    def remote(src, dst, ss, rs, dev):
        return pltpu.make_async_remote_copy(
            src_ref=src, dst_ref=dst, send_sem=ss, recv_sem=rs,
            device_id={"span": dev}, device_id_type=pl.DeviceIdType.MESH,
        )

    total = wq_hbm.shape[1]
    full = total // BLK
    rest = total - full * BLK

    def wcopy(b):
        cols = slice(b * BLK, min(b * BLK + BLK, total))
        return pltpu.make_async_copy(wq_hbm.at[:, cols], wq.at[:, cols], wsem.at[b])

    def hcopy(i):
        cols = pl.ds(i * LANE if isinstance(i, int) else pl.multiple_of(i * LANE, LANE), LANE)
        return pltpu.make_async_copy(hid_hbm.at[:, cols], hidt.at[:, cols], hsem.at[i])

    for i in range(toks // LANE):
        hcopy(i).start()
    smalls = [
        pltpu.make_async_copy(src, dst, isem.at[i])
        for i, (src, dst) in enumerate([
            (span_hbm, span_ref), (vw_hbm, vw), (map_hbm, map_ref), (noisy_hbm, noisy),
            (gain_hbm, gain), (w1_hbm, w1),
        ])
    ]
    for copy in smalls[:2]:
        copy.start()
    ocopy = pltpu.make_async_copy(wo_hbm, wo.at[koff : koff + inner], lsem.at[1])
    w2copy = pltpu.make_async_copy(w2_hbm, w2, lsem.at[2])
    pending = [wcopy(full)] if rest else []
    pending += [wcopy(b) for b in range(lo, full)] + smalls[2:] + [wcopy(b) for b in range(lo)] + [ocopy, w2copy]

    def fetch(count):
        for copy in pending[:count]:
            copy.start()
        del pending[:count]

    fetch(AHEAD)

    barrier = pltpu.get_barrier_semaphore()
    for k in range(1, n):
        pl.semaphore_signal(
            barrier, inc=1, device_id={"span": lax.rem(me + k, n)},
            device_id_type=pl.DeviceIdType.MESH,
        )

    def clear(ref, row0, row1, dtype):
        if row1 > row0:
            ref[row0:row1, :] = jnp.zeros((row1 - row0, ref.shape[1]), dtype)

    for ref, dtype in ((qt, BF), (vt, BF), (numt, F32), (wo, BF)):
        clear(ref, 0, koff, dtype)
        clear(ref, koff + inner, kw, dtype)

    for j in (0, kw // BLK - 1):
        dent[j] = jnp.zeros((8, toks), F32)

    for copy in smalls[:2]:
        copy.wait()
    span_row = span_ref[...].astype(F32)
    span_col = jnp.transpose(jnp.broadcast_to(span_row, (LANE, toks)))[:, 0:1]
    first_seg = span_row[:, 0:1]
    last_seg = span_row[:, toks - 1 : toks]
    lasts = [span_row[:, (c + 1) * chunk - 1 : (c + 1) * chunk] for c in range(2)]
    for c in range(2):
        rs = slice(c * chunk, (c + 1) * chunk)
        sr = span_row[:, rs]
        keep[c] = ((span_col[rs, :] <= sr) & (sr < lasts[c])).astype(F32).astype(BF)
    vwt[...] = jnp.concatenate([jnp.transpose(vw[...]), jnp.zeros((d, LANE - HDIM), F32).astype(BF)], axis=1)

    def turn(i, c):
        cols = pl.ds(pl.multiple_of(i * LANE, LANE), LANE)
        hcopy(i).wait()
        hid[cols, :] = jnp.transpose(hidt[:, cols])
        return c

    lax.fori_loop(0, toks // LANE, turn, 0)
    fetch(2)

    if rest:
        wcopy(full).wait()
        tail_w = jnp.transpose(wq[:, full * BLK : total])
        row = full * BLK - 2 * inner + koff
        vt[row : row + rest, :] = dot(tail_w, hidt[...]).astype(BF)

    def finish(out, b, rs):
        begin, end = b * BLK, b * BLK + BLK
        if begin < 2 * inner:
            pos = jnp.maximum(out, jnp.zeros_like(out))
            if end > 2 * inner:
                pos = jnp.where(iota(out.shape, 1) < 2 * inner - begin, pos, out)
            out = pos
        if end > inner and begin < 2 * inner:
            kp[rs, begin - lo * BLK : end - lo * BLK] = out
        if begin < inner:
            rows = min(end, inner) - begin
            qt[koff + begin : koff + begin + rows, rs] = jnp.transpose(out)[:rows]
        if end > 2 * inner:
            skip = max(2 * inner - begin, 0)
            row = begin + skip - 2 * inner + koff
            vt[row : row + BLK - skip, rs] = jnp.transpose(out)[skip:]

    def project(blocks):
        for b in blocks:
            wcopy(b).wait()
        fetch(3)
        for at, b in enumerate(blocks):
            cols = slice(b * BLK, b * BLK + BLK)
            pair = len(blocks) % 2 == 1 and at == len(blocks) - 1
            for rs in [slice(0, chunk), slice(chunk, toks)] if pair else [slice(0, toks)]:
                finish(dot(hid[rs, :], wq[:, cols]).astype(BF), b, rs)

    early = list(range(lo, full))
    for at in range(0, len(early) - 1, 2):
        project(early[at : at + (2 if at + 3 < len(early) else 3)])
    for copy in smalls[2:]:
        copy.wait()

    ones16 = jnp.ones((16, chunk), F32).astype(BF)
    lead_row = (span_row == first_seg).astype(F32).astype(BF)
    b0_row = (span_row[:, chunk:] <= lasts[0]).astype(F32).astype(BF)
    lane_slot = iota((HDIM, LANE), 1) // HDIM

    def diag(res, t):
        parts = [res[(t * PER + i) * HDIM : (t * PER + i + 1) * HDIM, t * LANE : (t + 1) * LANE] for i in range(PER)]
        out = parts[PER - 1]
        for i in range(PER - 2, -1, -1):
            out = jnp.where(lane_slot == i, parts[i], out)
        return out

    for j in range(tiles // 2):
        cols = slice(j * BLK, (j + 1) * BLK)
        res = []
        for c in range(2):
            rs = slice(c * chunk, (c + 1) * chunk)
            k8 = kp[rs, cols]
            lhs = jnp.concatenate([vt[cols, rs], ones16], axis=0)
            res.append(dot(lhs, k8))
            res.append(dot(lhs * lead_row[:, rs], k8))
            if c == 1:
                res.append(dot(lhs * b0_row, k8))
        c0, l0, c1, l1, b0 = res
        for t in range(2):
            u = 2 * j + t
            s0 = diag(c0, t)
            st_c0[u] = s0
            st_b0[u] = s0 + diag(b0, t)
            st_all[u] = s0 + diag(c1, t)
            st_lead[u] = diag(l0, t) + diag(l1, t)
            at = slice(t * LANE, (t + 1) * LANE)
            one = slice(BLK, BLK + 1)
            sum_c0[0, u : u + 1, :] = c0[one, at]
            sum_b0[0, u : u + 1, :] = c0[one, at] + b0[one, at]
            sum_c0[1, u : u + 1, :] = c0[one, at] + c1[one, at]
            sum_b0[1, u : u + 1, :] = l0[one, at] + l1[one, at]

    row_no = iota((half, LANE), 0)
    last_tile = tiles - 1

    def pack(dst, src, sums):
        for u in range(last_tile):
            full_unit = src[u] + src[last_tile] if u == 0 else src[u]
            for x in range(2):
                dst[2 * u + x] = full_unit[x * half : (x + 1) * half].astype(BF)
        sums = jnp.where(row_no < tiles, sums, 0.0)
        high = sums.astype(BF).astype(F32)
        low = sums - high
        high = jnp.where(row_no == half - 1, jnp.broadcast_to(first_seg, (half, LANE)), high)
        dst[2 * last_tile] = high.astype(BF)
        dst[2 * last_tile + 1] = low.astype(BF)
        for u in range(2 * tiles, 2 * units):
            dst[u] = jnp.zeros((half, LANE), F32).astype(BF)

    pack(st_send, st_all, sum_c0[1])
    pack(lead_send, st_lead, sum_b0[1])

    pl.semaphore_wait(barrier, n - 1)

    def part_copy(k):
        to = lax.rem(mate + k, TEAM)
        return remote(
            st_send.at[pl.ds(part * to, part)], part_recv.at[mate],
            psend.at[k], precv.at[mate], team * TEAM + to,
        )

    for k in range(1, TEAM):
        part_copy(k).start()

    def lead_copy(k):
        return remote(
            lead_send, lead_recv.at[k], lead_ssem.at[k], lead_rsem.at[k],
            lax.rem(me - 1 - k + n, n),
        )

    mine = map_ref[:, pl.ds(pl.multiple_of(me * toks, toks), toks)]
    target = mine // toks
    for b in range(n):
        map_rows[b : b + 1, :] = map_ref[:, b * toks : (b + 1) * toks]
    goal = map_rows[...] // toks
    where_in = map_rows[...] - goal * toks
    hits = [iota((n, toks), 0) == jnp.broadcast_to(target, (n, toks))]
    hits += [goal == me - 1 + x for x in range(3)]
    upper = (iota((toks, toks), 0) <= iota((toks, toks), 1)).astype(BF)
    cum = dot(jnp.concatenate([h.astype(F32) for h in hits], axis=0).astype(BF), upper)
    rank = jnp.sum(jnp.where(hits[0], cum[:n], 0.0), axis=0, keepdims=True).astype(jnp.int32) - 1
    packed = n * rows_to
    slot = rank // rows_to * packed + target * rows_to + lax.rem(rank, rows_to)
    onehot[...] = (iota((toks, toks), 0) == jnp.broadcast_to(slot, (toks, toks))).astype(F32).astype(BF)
    spot_f = where_in.astype(F32)
    lane_n = iota((n, LANE), 1)
    found = []
    for x in range(3):
        order = jnp.where(hits[1 + x], cum[n * (1 + x) : n * (2 + x)], 0.0)
        table = jnp.zeros((n, LANE), F32)
        for r in range(share):
            one = jnp.sum(jnp.where(order == float(r + 1), spot_f, 0.0), axis=1, keepdims=True)
            table = jnp.where(lane_n == r, one, table)
        whole_pos = table.astype(jnp.int32)
        found.append((whole_pos // IW).astype(F32))
        found.append(lax.rem(whole_pos, IW).astype(F32))
    slot_no = iota((LANE, toks), 1)
    rank_of = slot_no // packed * rows_to + lax.rem(slot_no, rows_to)
    spread = (iota((LANE, toks), 0) == rank_of).astype(F32).astype(BF)
    filled = dot(jnp.concatenate(found, axis=0).astype(BF), spread)
    source = lax.rem(iota((n, toks), 1), packed) // rows_to
    owned = iota((n, toks), 0) == source
    edge = 2 * IW
    starts = (0, edge, edge + toks)
    sizes = (edge, toks, edge)
    for x in range(3):
        lines, spots = [
            jnp.sum(jnp.where(owned, filled[n * (2 * x + y) : n * (2 * x + y + 1)], 0.0), axis=0, keepdims=True)
            for y in range(2)
        ]
        pos = (lines * float(IW) + spots).astype(jnp.int32)
        if x == 0:
            pos = pos - (toks - edge)
        place[starts[x] : starts[x] + sizes[x], :] = (
            iota((sizes[x], toks), 0) == jnp.broadcast_to(pos, (sizes[x], toks))
        ).astype(F32).astype(BF)
    for x in (0, n + 1):
        outgoing[x] = jnp.zeros((rows_to, LANE), F32).astype(BF)
    noisy_t[...] = jnp.concatenate(
        [jnp.transpose(noisy[...]), jnp.zeros((toks, LANE - HDIM), F32)], axis=1
    )

    fetch(len(pending))
    project(list(range(lo // 2)))

    part_recv[mate] = st_send[pl.ds(part * mate, part)]
    for k in range(1, TEAM):
        src = lax.rem(mate + k, TEAM)
        remote(
            st_send.at[pl.ds(0, part)], part_recv.at[src], psend.at[k], precv.at[src], team * TEAM + src
        ).wait_recv()
    whole = part_recv[0].astype(F32)
    for src in range(1, TEAM):
        whole = whole + part_recv[src].astype(F32)
    plane_send[...] = whole.astype(BF)

    def plane_copy(to):
        return remote(
            plane_send, plane_recv.at[team], gsend.at[to], grecv.at[team], TEAM * to + mate
        )

    for to in range(teams - 1, 0, -1):

        @pl.when(team < to)
        def _(to=to):
            plane_copy(to).start()

    for k in range(2):

        @pl.when(me >= k + 1)
        def _(k=k):
            lead_copy(k).start()

    project(list(range(lo // 2, lo)))

    def attend(jobs):
        def place(j, s):
            t, i = s // PER, s % PER
            if isinstance(j, int):
                return pl.ds(j * BLK + s * HDIM, HDIM), pl.ds(j * BLK + t * LANE, LANE), i
            return (
                pl.ds(pl.multiple_of(j * BLK + s * HDIM, HDIM), HDIM),
                pl.ds(pl.multiple_of(j * BLK + t * LANE, LANE), LANE), i,
            )

        def scores(j, s, c):
            rs = slice(c * chunk, (c + 1) * chunk)
            head, tile, i = place(j, s)
            pieces = [qt[head, rs]]
            if i:
                pieces = [jnp.zeros((i * HDIM, chunk), BF)] + pieces
            if i < PER - 1:
                pieces = pieces + [jnp.zeros(((PER - 1 - i) * HDIM, chunk), BF)]
            return dot(kp[rs, tile], jnp.concatenate(pieces, axis=0)).astype(BF) * keep[c]

        def values(j, s, c, score):
            rs = slice(c * chunk, (c + 1) * chunk)
            head, _, _ = place(j, s)
            out = dot(jnp.concatenate([vt[head, rs], ones16], axis=0), score)
            numt[head, rs] = out[:HDIM]
            dent[j, s : s + 1, rs] = out[HDIM : HDIM + 1]

        queue = []
        for job in jobs:
            queue.append((job, scores(*job)))
            if len(queue) > LAG:
                old, score = queue.pop(0)
                values(*old, score)
        for old, score in queue:
            values(*old, score)

    slots_of = BLK // HDIM
    groups = kw // BLK
    plain, extra = [], []
    for j in range(groups):
        slots = [s for s in range(slots_of) if first_slot <= j * slots_of + s < last_slot]
        if len(slots) == slots_of:
            plain.append(j)
        else:
            extra += [(j, s, c) for s in slots for c in range(2)]
    attend(extra)

    def attend_loop(j, carry_in):
        attend([(j, s, c) for s in range(slots_of) for c in range(2)])
        return carry_in

    lax.fori_loop(plain[0], plain[-1], attend_loop, 0)

    base[...] = jnp.zeros_like(base)
    for src in range(teams - 1):

        @pl.when(src < team)
        def _(src=src):
            remote(
                plane_send, plane_recv.at[src], gsend.at[src], grecv.at[src], TEAM * src + mate
            ).wait_recv()
            base[...] = base[...] + plane_recv[src].astype(F32)

    run = base[...]
    for m in range(TEAM):
        fin_send[m] = run.astype(BF)
        if m < TEAM - 1:
            run = run + part_recv[m].astype(F32)

    def fin_copy(k):
        to = lax.rem(mate + k, TEAM)
        return remote(
            fin_send.at[to], fin_recv.at[mate], fsend.at[k], frecv.at[mate], team * TEAM + to
        )

    for k in range(1, TEAM):
        fin_copy(k).start()

    lax.fori_loop(plain[-1], plain[-1] + 1, attend_loop, 0)

    tails = [span_row[:, c * chunk : (c + 1) * chunk] == lasts[c] for c in range(2)]
    masks = [(lane_slot == i).astype(F32).astype(BF) for i in range(PER)]
    den_slot = iota((half, LANE), 0)
    den_live = lax.rem(den_slot, PER) == iota((half, LANE), 1) // HDIM

    def left_side(states, sums):
        rows = []
        for state in states:
            state = state.astype(BF)
            rows += [state * m for m in masks]
        levels = []
        for total_sum in sums:
            high = total_sum.astype(BF).astype(F32)
            levels += [high, total_sum - high]
        den = jnp.broadcast_to(levels[-1], (half, LANE))
        for x in range(len(levels) - 2, -1, -1):
            den = jnp.where(den_slot < PER * (x + 1), levels[x], den)
        live = den_live & (den_slot < PER * len(levels))
        return jnp.concatenate(rows + [jnp.where(live, den, 0.0).astype(BF)], axis=0)

    def inside(j, carry_in):
        work = []
        for t in range(2):
            u = 2 * j + t
            tile = pl.ds(pl.multiple_of(j * BLK + t * LANE, LANE), LANE)
            one = pl.ds(u, 1)
            lhs = [
                left_side([st_b0[u]], [sum_b0[0, one, :]]),
                left_side([st_c0[u], st_all[u]], [sum_c0[0, one, :], sum_c0[1, one, :]]),
            ]
            for c in range(2):
                rs = slice(c * chunk, (c + 1) * chunk)
                work.append((t, c, tile, rs, dot(lhs[c], qt[tile, rs])))
        for t, c, tile, rs, res in work:
            tail = jnp.broadcast_to(tails[c], (LANE, chunk))
            d_all = res[LANE * (c + 1) :]
            d_one = d_all[:PER] + d_all[PER : 2 * PER]
            if c == 0:
                more, d_more = jnp.where(tail, res[:LANE], 0.0), jnp.where(tail[:PER], d_one, 0.0)
            else:
                d_two = d_all[2 * PER : 3 * PER] + d_all[3 * PER :]
                more, d_more = jnp.where(tail, res[LANE : 2 * LANE], res[:LANE]), jnp.where(tail[:PER], d_two, d_one)
            numt[tile, rs] = numt[tile, rs] + more
            dent[j, t * PER : (t + 1) * PER, rs] = dent[j, t * PER : (t + 1) * PER, rs] + d_more
        return carry_in

    lax.fori_loop(0, groups, inside, 0)

    after[...] = jnp.zeros_like(after)
    for k in range(2):

        @pl.when(me + 1 + k < n)
        def _(k=k):
            remote(
                lead_send, lead_recv.at[k], lead_ssem.at[k], lead_rsem.at[k], lax.rem(me + 1 + k, n)
            ).wait_recv()
            same = (lead_recv[k, 2 * last_tile, half - 1 : half, 0:1].astype(F32) == last_seg).astype(F32)
            after[...] = after[...] + lead_recv[k].astype(F32) * same

    fin_recv[mate] = fin_send[mate]
    for k in range(1, TEAM):
        src = lax.rem(mate + k, TEAM)
        remote(
            fin_send.at[0], fin_recv.at[src], fsend.at[k], frecv.at[src], team * TEAM + src
        ).wait_recv()
    for m in range(TEAM):
        carry[m * part : (m + 1) * part] = fin_recv[m].astype(F32)

    reach_row = jnp.concatenate(
        [(tails[c] & (lasts[c] == last_seg)).astype(F32) for c in range(2)], axis=1
    )

    def unit_of(ref, u):
        u = 0 if u == last_tile else u
        return jnp.concatenate([ref[2 * u], ref[2 * u + 1]], axis=0)

    def sums_of(ref, u):
        return ref[2 * last_tile, u : u + 1, :] + ref[2 * last_tile + 1, u : u + 1, :]

    def outside(j):
        out = []
        for t in range(2):
            u = 2 * j + t
            lhs = left_side([unit_of(carry, u), unit_of(after, u)], [sums_of(carry, u), sums_of(after, u)])
            out.append(dot(lhs, qt[u * LANE : (u + 1) * LANE, :]))
        return out

    def close(j, parts):
        rows = []
        for t, res in enumerate(parts):
            u = 2 * j + t
            reach = jnp.broadcast_to(reach_row, (LANE, toks))
            numer = numt[u * LANE : (u + 1) * LANE, :] + res[:LANE] + reach * res[LANE : 2 * LANE]
            d_all = res[2 * LANE :]
            den = d_all[:PER] + d_all[PER : 2 * PER] + reach[:PER] * (d_all[2 * PER : 3 * PER] + d_all[3 * PER :])
            inv = 1.0 / (1.0 + dent[j, t * PER : (t + 1) * PER, :] + den)
            rows += [(numer[i * HDIM : (i + 1) * HDIM] * inv[i : i + 1]).astype(BF) for i in range(PER)]
        att[:, j * BLK : (j + 1) * BLK] = jnp.transpose(jnp.concatenate(rows, axis=0))

    held = outside(0)
    for j in range(1, groups):
        coming = outside(j)
        close(j - 1, held)
        held = coming
    close(groups - 1, held)

    ocopy.wait()
    square = jnp.zeros((toks, LANE), F32)

    def rise(b):
        end = min(b + BLK, d)
        if d - b > BLK:
            return dot(att[...], wo[:, b:end])
        return jnp.concatenate([dot(att[:chunk, :], wo[:, b:end]), dot(att[chunk:, :], wo[:, b:end])], axis=0)

    def settle(b, part_sum, square):
        end = min(b + BLK, d)
        mixed = hid[:, b:end].astype(F32) + part_sum
        sq = mixed * mixed
        for x in range(0, end - b, LANE):
            width = min(LANE, end - b - x)
            piece = sq[:, x : x + width]
            if width < LANE:
                piece = jnp.concatenate([piece, jnp.zeros((toks, LANE - width), F32)], axis=1)
            square = square + piece
        ybuf[:, b:end] = (mixed * jnp.broadcast_to(gain[b:end][None, :], mixed.shape)).astype(BF)
        return square

    for b in range(0, d, BLK):
        square = settle(b, rise(b), square)
    vel = dot(ybuf[...], vwt[...])
    meansq = jnp.sum(square, axis=1, keepdims=True) * (1.0 / d)
    lat = noisy_t[...] - vel * (0.5 * lax.rsqrt(meansq + 1e-06))
    noisy_t[...] = lat
    sorted_lat = dot(onehot[...], lat.astype(BF))
    dense = sorted_lat[:packed]
    for a in range(1, PER):
        dense = dense + pltpu.roll(sorted_lat[a * packed : (a + 1) * packed], a * HDIM, 1)
    outgoing[1 : n + 1] = dense.reshape(n, rows_to, LANE).astype(BF)

    def flip(k):
        to, bit = 0, 1
        while bit < n:
            have = lax.rem(me // bit, 2)
            to = to + bit * (1 - have if k & bit else have)
            bit *= 2
        return to

    def out_copy(k):
        to = flip(k)
        return remote(outgoing.at[pl.ds(to, 3)], incoming.at[me], asend.at[k], arecv.at[me], to)

    for k in range(n - 1, 0, -1):
        out_copy(k).start()
    incoming[me] = outgoing[pl.ds(me, 3)]
    lat_out[...] = jnp.transpose(noisy_t[...])[:HDIM]
    for k in range(1, n):
        src = flip(k)
        remote(outgoing.at[pl.ds(0, 3)], incoming.at[src], asend.at[k], arecv.at[src], src).wait_recv()

    for x in range(3):
        dense = incoming[:, x].astype(F32).reshape(packed, LANE)
        slots = [dense] + [pltpu.roll(dense, LANE - a * HDIM, 1) for a in range(1, PER)]
        at = slice(starts[x], starts[x] + sizes[x])
        wide[at, :] = dot(place[at, :], jnp.concatenate(slots, axis=0).astype(BF))

    ext = toks + 2 * edge
    x = wide[...]
    column = lax.rem(iota((ext, 128), 0), IW)
    lane = iota((ext, 128), 1)
    left = jnp.where(column == 0, 0.0, pltpu.roll(x, 1, 0))
    right = jnp.where(column == IW - 1, 0.0, pltpu.roll(x, ext - 1, 0))
    three = jnp.where(
        lane < HDIM, left,
        jnp.where(lane < 2 * HDIM, pltpu.roll(x, HDIM, 1),
                  jnp.where(lane < 3 * HDIM, pltpu.roll(right, 2 * HDIM, 1), 0.0)),
    )
    three = three.astype(BF)
    mid = toks + 2 * IW
    k3 = 3 * HDIM
    acc = dot(three[0:mid, :k3], w1[0])
    acc = acc + dot(three[IW : IW + mid, :k3], w1[1])
    acc = acc + dot(three[2 * IW : 2 * IW + mid, :k3], w1[2])
    feat = acc / (1.0 + jnp.exp(-acc))
    row_at = iota((mid, 1), 0) // IW
    outside = ((row_at == 0) & (me == 0)) | ((row_at == mid // IW - 1) & (me == n - 1))
    feat = jnp.where(outside, 0.0, feat).astype(BF).astype(F32)
    column = lax.rem(iota((mid, 1), 0), IW)
    shifted[1] = feat.astype(BF)
    shifted[0] = jnp.where(column == 0, 0.0, pltpu.roll(feat, 1, 0)).astype(BF)
    shifted[2] = jnp.where(column == IW - 1, 0.0, pltpu.roll(feat, mid - 1, 0)).astype(BF)
    w2copy.wait()
    out = None
    for a in range(3):
        for b in range(3):
            piece = dot(shifted[b, a * IW : a * IW + toks, :], w2[3 * a + b])
            out = piece if out is None else out + piece
    dec_out[...] = out.astype(BF)

    for k in range(1, TEAM):
        part_copy(k).wait_send()
        fin_copy(k).wait_send()

    for k in range(2):

        @pl.when(me >= k + 1)
        def _(k=k):
            lead_copy(k).wait_send()

    for to in range(1, teams):

        @pl.when(team < to)
        def _(to=to):
            plane_copy(to).wait_send()

    for k in range(1, n):
        out_copy(k).wait_send()


def flush(lat, dec, lat_out, dec_out, sem):
    copies = [
        pltpu.make_async_copy(dec, dec_out, sem.at[0]),
        pltpu.make_async_copy(lat, lat_out, sem.at[1]),
    ]
    for copy in copies:
        copy.start()
    for copy in copies:
        copy.wait()


def body(
    hidden_in, noisy_latents, span_ids, tile_map, qkv_weight, out_weight,
    norm_gain, velocity_weight, conv_first, conv_second,
):
    toks, d = hidden_in.shape
    inner = out_weight.shape[0]
    n = lax.axis_size("span")
    ch = conv_first.shape[3]
    chunk = toks // 2
    lo = inner // BLK
    koff = inner - lo * BLK
    kw = -(-(koff + inner) // BLK) * BLK
    tiles = kw // LANE
    units = -(-2 * tiles // TEAM) * TEAM // 2
    part = 2 * units // TEAM
    teams = n // TEAM
    edge = 2 * IW
    mid = toks + 2 * IW
    blocks = -(-qkv_weight.shape[1] // BLK)
    vm, dma = pltpu.VMEM, pltpu.SemaphoreType.DMA
    any_, vmem = pl.BlockSpec(memory_space=pl.ANY), pl.BlockSpec(memory_space=pltpu.VMEM)
    maps = tile_map.shape[0]
    half = HDIM // 2
    rows_to = toks // n // PER
    scratch = [
        vm((HDIM, toks), F32), vm((1, toks), jnp.int32), vm((1, maps), jnp.int32),
        vm((d,), F32), vm((HDIM, d), BF), vm((3, 3 * HDIM, ch), BF),
        vm((d, toks), BF), vm((toks, d), BF), vm(qkv_weight.shape, BF), vm((kw, d), BF),
        vm((9, ch, ch), BF),
        vm((kw, toks), BF), vm((toks, kw), BF), vm((kw, toks), BF),
        vm((kw, toks), F32), vm((kw // BLK, 8, toks), F32), vm((2, chunk, chunk), BF),
        vm((toks, kw), BF), vm((toks, d), BF), vm((d, LANE), BF),
        vm((tiles, HDIM, LANE), F32), vm((tiles, HDIM, LANE), F32),
        vm((tiles, HDIM, LANE), F32), vm((tiles, HDIM, LANE), F32),
        vm((2, half, LANE), F32), vm((2, half, LANE), F32),
        vm((2 * units, half, LANE), BF), vm((2 * units, half, LANE), BF), vm((2, 2 * units, half, LANE), BF),
        vm((TEAM, part, half, LANE), BF), vm((part, half, LANE), BF), vm((teams, part, half, LANE), BF),
        vm((TEAM, part, half, LANE), BF), vm((TEAM, part, half, LANE), BF),
        vm((part, half, LANE), F32), vm((2 * units, half, LANE), F32), vm((2 * units, half, LANE), F32),
        vm((toks, toks), BF), vm((n, toks), jnp.int32), vm((toks + 2 * edge, toks), BF), vm((toks, LANE), F32),
        vm((n + 2, rows_to, LANE), BF), vm((n, 3, rows_to, LANE), BF),
        vm((toks + 2 * edge, 128), F32),
        vm((3, mid, ch), BF),
        dma((blocks,)), dma((3,)), dma((toks // LANE,)), dma((6,)), dma((TEAM,)), dma((TEAM,)), dma((teams,)), dma((teams,)),
        dma((TEAM,)), dma((TEAM,)),
        dma((2,)), dma((2,)), dma((n,)), dma((n,)),
    ]
    latents, decoded = pl.pallas_call(
        functools.partial(kernel, (n, toks, d, inner)),
        out_shape=(
            pltpu.VMEM(noisy_latents.shape[::-1], F32),
            pltpu.VMEM((toks, ch), BF),
        ),
        in_specs=[any_] * 10,
        out_specs=(vmem, vmem),
        scratch_shapes=scratch,
        compiler_params=pltpu.CompilerParams(
            collective_id=0, has_side_effects=True, vmem_limit_bytes=60 * 1024 * 1024
        ),
    )(
        hidden_in.T, noisy_latents.T, span_ids.reshape(1, toks), tile_map.reshape(1, -1),
        qkv_weight, out_weight, norm_gain, velocity_weight.T,
        conv_first.reshape(3, 3 * HDIM, ch), conv_second.reshape(9, ch, ch),
    )
    latents, decoded = [pltpu.with_memory_space_constraint(x, pltpu.VMEM) for x in (latents, decoded)]
    latents, decoded = pl.pallas_call(
        flush,
        out_shape=(
            jax.ShapeDtypeStruct(latents.shape, F32),
            jax.ShapeDtypeStruct(decoded.shape, BF),
        ),
        in_specs=[vmem, vmem],
        out_specs=(any_, any_),
        scratch_shapes=[dma((2,))],
    )(latents, decoded)
    return latents.T, decoded.reshape(toks // IW, IW, ch)


def solution(mesh):
    rows = P(("groups", "span"), None)
    placed = (rows, rows, P(("groups", "span")), P("groups")) + (P(),) * 6
    return jax.shard_map(
        body, mesh=mesh, in_specs=placed,
        out_specs=(rows, P(("groups", "span"), None, None)), check_vma=False,
    )
```

```python
import functools

import jax
import jax.numpy as jnp
from jax import lax
from jax.experimental import pallas as pl
from jax.experimental.pallas import tpu as pltpu
from jax.sharding import PartitionSpec as P

HDIM = 32
IW = 64
BLK = 256
LANE = 128
PER = LANE // HDIM
TEAM = 4
LAG = 3
AHEAD = 4
BF = jnp.bfloat16
F32 = jnp.float32


def dot(a, b):
    return jnp.dot(a, b, preferred_element_type=F32)


def dot_nt(a, b):
    return lax.dot_general(a, b, (((1,), (1,)), ((), ())), preferred_element_type=F32)


def iota(shape, axis):
    return lax.broadcasted_iota(jnp.int32, shape, axis)


def kernel(
    cfg,
    hid_hbm, noisy_hbm, span_hbm, map_hbm, wq_hbm, wo_hbm, gain_hbm, vw_hbm, w1_hbm, w2_hbm,
    lat_out, dec_out,
    noisy, span_ref, map_ref, gain, vw, w1,
    hidt, hid, wq, wo, w2, qt, kp, vt, numt, dent, keep, att, ybuf, vwt,
    st_c0, st_b0, st_all, st_lead, sum_c0, sum_b0, st_send, lead_send, lead_recv,
    part_recv, plane_send, plane_recv, fin_send, fin_recv, base, carry, after, onehot, map_rows, place, noisy_t, outgoing, incoming,
    wide, shifted,
    wsem, lsem, hsem, isem, psend, precv, gsend, grecv, fsend, frecv, lead_ssem, lead_rsem, asend, arecv,
):
    n, toks, d, inner = cfg
    me = lax.axis_index("span")
    mate = lax.rem(me, TEAM)
    team = me // TEAM
    teams = n // TEAM
    share = toks // n
    rows_to = share // PER
    chunk = toks // 2
    lo = inner // BLK
    koff = inner - lo * BLK
    kw = kp.shape[1]
    tiles = kw // LANE
    units = st_send.shape[0] // 2
    part = 2 * units // TEAM
    half = HDIM // 2
    heads = inner // HDIM
    first_slot = koff // HDIM
    last_slot = first_slot + heads

    def remote(src, dst, ss, rs, dev):
        return pltpu.make_async_remote_copy(
            src_ref=src, dst_ref=dst, send_sem=ss, recv_sem=rs,
            device_id={"span": dev}, device_id_type=pl.DeviceIdType.MESH,
        )

    total = wq_hbm.shape[1]
    full = total // BLK
    rest = total - full * BLK

    def wcopy(b):
        cols = slice(b * BLK, min(b * BLK + BLK, total))
        return pltpu.make_async_copy(wq_hbm.at[:, cols], wq.at[:, cols], wsem.at[b])

    def hcopy(i):
        cols = pl.ds(i * LANE if isinstance(i, int) else pl.multiple_of(i * LANE, LANE), LANE)
        return pltpu.make_async_copy(hid_hbm.at[:, cols], hidt.at[:, cols], hsem.at[i])

    for i in range(toks // LANE):
        hcopy(i).start()
    smalls = [
        pltpu.make_async_copy(src, dst, isem.at[i])
        for i, (src, dst) in enumerate([
            (span_hbm, span_ref), (vw_hbm, vw), (map_hbm, map_ref), (noisy_hbm, noisy),
            (gain_hbm, gain), (w1_hbm, w1),
        ])
    ]
    for copy in smalls[:2]:
        copy.start()
    ocopy = pltpu.make_async_copy(wo_hbm, wo.at[koff : koff + inner], lsem.at[1])
    w2copy = pltpu.make_async_copy(w2_hbm, w2, lsem.at[2])
    pending = [wcopy(full)] if rest else []
    pending += [wcopy(b) for b in range(lo, full)] + smalls[2:] + [wcopy(b) for b in range(lo)] + [ocopy, w2copy]

    def fetch(count):
        for copy in pending[:count]:
            copy.start()
        del pending[:count]

    fetch(AHEAD)

    barrier = pltpu.get_barrier_semaphore()
    for k in range(1, n):
        pl.semaphore_signal(
            barrier, inc=1, device_id={"span": lax.rem(me + k, n)},
            device_id_type=pl.DeviceIdType.MESH,
        )

    def clear(ref, row0, row1, dtype):
        if row1 > row0:
            ref[row0:row1, :] = jnp.zeros((row1 - row0, ref.shape[1]), dtype)

    for ref, dtype in ((qt, BF), (vt, BF), (numt, F32), (wo, BF)):
        clear(ref, 0, koff, dtype)
        clear(ref, koff + inner, kw, dtype)

    for j in (0, kw // BLK - 1):
        dent[j] = jnp.zeros((8, toks), F32)

    for copy in smalls[:2]:
        copy.wait()
    span_row = span_ref[...].astype(F32)
    span_col = jnp.transpose(jnp.broadcast_to(span_row, (LANE, toks)))[:, 0:1]
    first_seg = span_row[:, 0:1]
    last_seg = span_row[:, toks - 1 : toks]
    lasts = [span_row[:, (c + 1) * chunk - 1 : (c + 1) * chunk] for c in range(2)]
    for c in range(2):
        rs = slice(c * chunk, (c + 1) * chunk)
        sr = span_row[:, rs]
        keep[c] = ((span_col[rs, :] <= sr) & (sr < lasts[c])).astype(F32).astype(BF)
    vwt[...] = jnp.concatenate([jnp.transpose(vw[...]), jnp.zeros((d, LANE - HDIM), F32).astype(BF)], axis=1)

    def turn(i, c):
        cols = pl.ds(pl.multiple_of(i * LANE, LANE), LANE)
        hcopy(i).wait()
        hid[cols, :] = jnp.transpose(hidt[:, cols])
        return c

    lax.fori_loop(0, chunk // LANE, turn, 0)
    fetch(2)

    def finish(out, b, rs):
        begin, end = b * BLK, b * BLK + BLK
        if begin < 2 * inner:
            pos = jnp.maximum(out, jnp.zeros_like(out))
            if end > 2 * inner:
                pos = jnp.where(iota(out.shape, 1) < 2 * inner - begin, pos, out)
            out = pos
        if end > inner and begin < 2 * inner:
            kp[rs, begin - lo * BLK : end - lo * BLK] = out
        if begin < inner:
            rows = min(end, inner) - begin
            qt[koff + begin : koff + begin + rows, rs] = jnp.transpose(out)[:rows]
        if end > 2 * inner:
            skip = max(2 * inner - begin, 0)
            row = begin + skip - 2 * inner + koff
            vt[row : row + BLK - skip, rs] = jnp.transpose(out)[skip:]

    def project(blocks, ready=False, spans=None):
        if not ready:
            for b in blocks:
                wcopy(b).wait()
            fetch(3)
        for at, b in enumerate(blocks):
            cols = slice(b * BLK, b * BLK + BLK)
            pair = len(blocks) % 2 == 1 and at == len(blocks) - 1
            for rs in spans or ([slice(0, chunk), slice(chunk, toks)] if pair else [slice(0, toks)]):
                finish(dot(hid[rs, :], wq[:, cols]).astype(BF), b, rs)

    def project_rest():
        tail_w = jnp.transpose(wq[:, full * BLK : total])
        row = full * BLK - 2 * inner + koff
        vt[row : row + rest, :] = dot(tail_w, hidt[...]).astype(BF)

    early = list(range(lo, full))
    for at in range(0, len(early) - 1, 2):
        blocks = early[at : at + (2 if at + 3 < len(early) else 3)]
        if at > 0:
            project(blocks)
            continue
        for b in blocks + ([full] if rest else []):
            wcopy(b).wait()
        for i in range(chunk // LANE, toks // LANE):
            hcopy(i).wait()
        fetch(3)
        project(blocks, ready=True, spans=[slice(0, chunk)])
        for i in range(chunk // LANE, toks // LANE):
            rows = slice(i * LANE, (i + 1) * LANE)
            hid[rows, :] = jnp.transpose(hidt[:, rows])
        if rest:
            project_rest()
        project(blocks, ready=True, spans=[slice(chunk, toks)])
    for copy in smalls[2:]:
        copy.wait()

    ones16 = jnp.ones((16, chunk), F32).astype(BF)
    lead_row = (span_row == first_seg).astype(F32).astype(BF)
    b0_row = (span_row[:, chunk:] <= lasts[0]).astype(F32).astype(BF)
    lane_slot = iota((HDIM, LANE), 1) // HDIM

    def diag(res, t):
        parts = [res[(t * PER + i) * HDIM : (t * PER + i + 1) * HDIM, t * LANE : (t + 1) * LANE] for i in range(PER)]
        out = parts[PER - 1]
        for i in range(PER - 2, -1, -1):
            out = jnp.where(lane_slot == i, parts[i], out)
        return out

    at_tile = [slice(0, LANE), slice(LANE, BLK)]
    one = slice(BLK, BLK + 1)

    def sides(j, c):
        cols, rs = slice(j * BLK, (j + 1) * BLK), slice(c * chunk, (c + 1) * chunk)
        return jnp.concatenate([vt[cols, rs], ones16], axis=0), kp[rs, cols]

    for j in range(tiles // 2):
        c0, c1 = [dot(*sides(j, c)) for c in range(2)]
        for t in range(2):
            u = 2 * j + t
            s0 = diag(c0, t)
            st_c0[u] = s0
            st_all[u] = s0 + diag(c1, t)
            sum_c0[0, u : u + 1, :] = c0[one, at_tile[t]]
            sum_c0[1, u : u + 1, :] = c0[one, at_tile[t]] + c1[one, at_tile[t]]

    row_no = iota((half, LANE), 0)
    last_tile = tiles - 1

    def pack(dst, src, sums):
        for u in range(last_tile):
            full_unit = src[u] + src[last_tile] if u == 0 else src[u]
            for x in range(2):
                dst[2 * u + x] = full_unit[x * half : (x + 1) * half].astype(BF)
        sums = jnp.where(row_no < tiles, sums, 0.0)
        high = sums.astype(BF).astype(F32)
        low = sums - high
        high = jnp.where(row_no == half - 1, jnp.broadcast_to(first_seg, (half, LANE)), high)
        dst[2 * last_tile] = high.astype(BF)
        dst[2 * last_tile + 1] = low.astype(BF)
        for u in range(2 * tiles, 2 * units):
            dst[u] = jnp.zeros((half, LANE), F32).astype(BF)

    pack(st_send, st_all, sum_c0[1])

    pl.semaphore_wait(barrier, n - 1)

    def part_copy(k):
        to = lax.rem(mate + k, TEAM)
        return remote(
            st_send.at[pl.ds(part * to, part)], part_recv.at[mate],
            psend.at[k], precv.at[mate], team * TEAM + to,
        )

    for k in range(1, TEAM):
        part_copy(k).start()

    def lead_copy(k):
        return remote(
            lead_send, lead_recv.at[k], lead_ssem.at[k], lead_rsem.at[k],
            lax.rem(me - 1 - k + n, n),
        )

    for j in range(tiles // 2):
        (v0, k0), (v1, k1) = sides(j, 0), sides(j, 1)
        l0, l1 = dot(v0 * lead_row[:, :chunk], k0), dot(v1 * lead_row[:, chunk:], k1)
        b0 = dot(v1 * b0_row, k1)
        for t in range(2):
            u = 2 * j + t
            st_b0[u] = st_c0[u] + diag(b0, t)
            st_lead[u] = diag(l0, t) + diag(l1, t)
            sum_b0[0, u : u + 1, :] = sum_c0[0, u : u + 1, :] + b0[one, at_tile[t]]
            sum_b0[1, u : u + 1, :] = l0[one, at_tile[t]] + l1[one, at_tile[t]]

    pack(lead_send, st_lead, sum_b0[1])

    fetch(len(pending))
    for b in range(lo // 2):
        wcopy(b).wait()
    mine = map_ref[:, pl.ds(pl.multiple_of(me * toks, toks), toks)]
    target = mine // toks
    for b in range(n):
        map_rows[b : b + 1, :] = map_ref[:, b * toks : (b + 1) * toks]
    goal = map_rows[...] // toks
    where_in = map_rows[...] - goal * toks
    hits = [iota((n, toks), 0) == jnp.broadcast_to(target, (n, toks))]
    hits += [goal == me - 1 + x for x in range(3)]
    upper = (iota((toks, toks), 0) <= iota((toks, toks), 1)).astype(BF)
    cum = dot(jnp.concatenate([h.astype(F32) for h in hits], axis=0).astype(BF), upper)
    rank = jnp.sum(jnp.where(hits[0], cum[:n], 0.0), axis=0, keepdims=True).astype(jnp.int32) - 1
    packed = n * rows_to
    slot = rank // rows_to * packed + target * rows_to + lax.rem(rank, rows_to)
    onehot[...] = (iota((toks, toks), 0) == jnp.broadcast_to(slot, (toks, toks))).astype(F32).astype(BF)
    project(list(range(lo // 2)), ready=True)
    spot_f = where_in.astype(F32)
    lane_n = iota((n, LANE), 1)
    found = []
    for x in range(3):
        order = jnp.where(hits[1 + x], cum[n * (1 + x) : n * (2 + x)], 0.0)
        table = jnp.zeros((n, LANE), F32)
        for r in range(share):
            one = jnp.sum(jnp.where(order == float(r + 1), spot_f, 0.0), axis=1, keepdims=True)
            table = jnp.where(lane_n == r, one, table)
        whole_pos = table.astype(jnp.int32)
        found.append((whole_pos // IW).astype(F32))
        found.append(lax.rem(whole_pos, IW).astype(F32))
    slot_no = iota((LANE, toks), 1)
    rank_of = slot_no // packed * rows_to + lax.rem(slot_no, rows_to)
    spread = (iota((LANE, toks), 0) == rank_of).astype(F32).astype(BF)
    filled = dot(jnp.concatenate(found, axis=0).astype(BF), spread)
    source = lax.rem(iota((n, toks), 1), packed) // rows_to
    owned = iota((n, toks), 0) == source
    edge = 2 * IW
    starts = (0, edge, edge + toks)
    sizes = (edge, toks, edge)
    for x in range(3):
        lines, spots = [
            jnp.sum(jnp.where(owned, filled[n * (2 * x + y) : n * (2 * x + y + 1)], 0.0), axis=0, keepdims=True)
            for y in range(2)
        ]
        pos = (lines * float(IW) + spots).astype(jnp.int32)
        if x == 0:
            pos = pos - (toks - edge)
        place[starts[x] : starts[x] + sizes[x], :] = (
            iota((sizes[x], toks), 0) == jnp.broadcast_to(pos, (sizes[x], toks))
        ).astype(F32).astype(BF)
    for x in (0, n + 1):
        outgoing[x] = jnp.zeros((rows_to, LANE), F32).astype(BF)
    noisy_t[...] = jnp.concatenate(
        [jnp.transpose(noisy[...]), jnp.zeros((toks, LANE - HDIM), F32)], axis=1
    )

    part_recv[mate] = st_send[pl.ds(part * mate, part)]
    for k in range(1, TEAM):
        src = lax.rem(mate + k, TEAM)
        remote(
            st_send.at[pl.ds(0, part)], part_recv.at[src], psend.at[k], precv.at[src], team * TEAM + src
        ).wait_recv()
    whole = part_recv[0].astype(F32)
    for src in range(1, TEAM):
        whole = whole + part_recv[src].astype(F32)
    plane_send[...] = whole.astype(BF)

    def plane_copy(to):
        return remote(
            plane_send, plane_recv.at[team], gsend.at[to], grecv.at[team], TEAM * to + mate
        )

    for to in range(teams - 1, 0, -1):

        @pl.when(team < to)
        def _(to=to):
            plane_copy(to).start()

    for k in range(2):

        @pl.when(me >= k + 1)
        def _(k=k):
            lead_copy(k).start()

    project(list(range(lo // 2, lo)))

    def attend(jobs):
        def place(j, s):
            t, i = s // PER, s % PER
            if isinstance(j, int):
                return pl.ds(j * BLK + s * HDIM, HDIM), pl.ds(j * BLK + t * LANE, LANE), i
            return (
                pl.ds(pl.multiple_of(j * BLK + s * HDIM, HDIM), HDIM),
                pl.ds(pl.multiple_of(j * BLK + t * LANE, LANE), LANE), i,
            )

        def scores(j, s, c):
            rs = slice(c * chunk, (c + 1) * chunk)
            head, tile, i = place(j, s)
            pieces = [qt[head, rs]]
            if i:
                pieces = [jnp.zeros((i * HDIM, chunk), BF)] + pieces
            if i < PER - 1:
                pieces = pieces + [jnp.zeros(((PER - 1 - i) * HDIM, chunk), BF)]
            return dot(kp[rs, tile], jnp.concatenate(pieces, axis=0)).astype(BF) * keep[c]

        def values(j, s, c, score):
            rs = slice(c * chunk, (c + 1) * chunk)
            head, _, _ = place(j, s)
            out = dot(jnp.concatenate([vt[head, rs], ones16], axis=0), score)
            numt[head, rs] = out[:HDIM]
            dent[j, s : s + 1, rs] = out[HDIM : HDIM + 1]

        queue = []
        for job in jobs:
            queue.append((job, scores(*job)))
            if len(queue) > LAG:
                old, score = queue.pop(0)
                values(*old, score)
        for old, score in queue:
            values(*old, score)

    slots_of = BLK // HDIM
    groups = kw // BLK
    plain, extra = [], []
    for j in range(groups):
        slots = [s for s in range(slots_of) if first_slot <= j * slots_of + s < last_slot]
        if len(slots) == slots_of:
            plain.append(j)
        else:
            extra += [(j, s, c) for s in slots for c in range(2)]
    attend(extra)

    def attend_loop(j, carry_in):
        attend([(j, s, c) for s in range(slots_of) for c in range(2)])
        return carry_in

    lax.fori_loop(plain[0], plain[-1], attend_loop, 0)

    base[...] = jnp.zeros_like(base)
    for src in range(teams - 1):

        @pl.when(src < team)
        def _(src=src):
            remote(
                plane_send, plane_recv.at[src], gsend.at[src], grecv.at[src], TEAM * src + mate
            ).wait_recv()
            base[...] = base[...] + plane_recv[src].astype(F32)

    run = base[...]
    for m in range(TEAM):
        fin_send[m] = run.astype(BF)
        if m < TEAM - 1:
            run = run + part_recv[m].astype(F32)

    def fin_copy(k):
        to = lax.rem(mate + k, TEAM)
        return remote(
            fin_send.at[to], fin_recv.at[mate], fsend.at[k], frecv.at[mate], team * TEAM + to
        )

    for k in range(1, TEAM):
        fin_copy(k).start()

    lax.fori_loop(plain[-1], plain[-1] + 1, attend_loop, 0)

    tails = [span_row[:, c * chunk : (c + 1) * chunk] == lasts[c] for c in range(2)]
    masks = [(lane_slot == i).astype(F32).astype(BF) for i in range(PER)]
    den_slot = iota((half, LANE), 0)
    den_live = lax.rem(den_slot, PER) == iota((half, LANE), 1) // HDIM

    def left_side(states, sums):
        rows = []
        for state in states:
            state = state.astype(BF)
            rows += [state * m for m in masks]
        levels = []
        for total_sum in sums:
            high = total_sum.astype(BF).astype(F32)
            levels += [high, total_sum - high]
        den = jnp.broadcast_to(levels[-1], (half, LANE))
        for x in range(len(levels) - 2, -1, -1):
            den = jnp.where(den_slot < PER * (x + 1), levels[x], den)
        live = den_live & (den_slot < PER * len(levels))
        return jnp.concatenate(rows + [jnp.where(live, den, 0.0).astype(BF)], axis=0)

    def inside(j, carry_in):
        work = []
        for t in range(2):
            u = 2 * j + t
            tile = pl.ds(pl.multiple_of(j * BLK + t * LANE, LANE), LANE)
            one = pl.ds(u, 1)
            lhs = [
                left_side([st_b0[u]], [sum_b0[0, one, :]]),
                left_side([st_c0[u], st_all[u]], [sum_c0[0, one, :], sum_c0[1, one, :]]),
            ]
            for c in range(2):
                rs = slice(c * chunk, (c + 1) * chunk)
                work.append((t, c, tile, rs, dot(lhs[c], qt[tile, rs])))
        for t, c, tile, rs, res in work:
            tail = jnp.broadcast_to(tails[c], (LANE, chunk))
            d_all = res[LANE * (c + 1) :]
            d_one = d_all[:PER] + d_all[PER : 2 * PER]
            if c == 0:
                more, d_more = jnp.where(tail, res[:LANE], 0.0), jnp.where(tail[:PER], d_one, 0.0)
            else:
                d_two = d_all[2 * PER : 3 * PER] + d_all[3 * PER :]
                more, d_more = jnp.where(tail, res[LANE : 2 * LANE], res[:LANE]), jnp.where(tail[:PER], d_two, d_one)
            numt[tile, rs] = numt[tile, rs] + more
            dent[j, t * PER : (t + 1) * PER, rs] = dent[j, t * PER : (t + 1) * PER, rs] + d_more
        return carry_in

    lax.fori_loop(0, groups, inside, 0)

    after[...] = jnp.zeros_like(after)
    for k in range(2):

        @pl.when(me + 1 + k < n)
        def _(k=k):
            remote(
                lead_send, lead_recv.at[k], lead_ssem.at[k], lead_rsem.at[k], lax.rem(me + 1 + k, n)
            ).wait_recv()
            same = (lead_recv[k, 2 * last_tile, half - 1 : half, 0:1].astype(F32) == last_seg).astype(F32)
            after[...] = after[...] + lead_recv[k].astype(F32) * same

    fin_recv[mate] = fin_send[mate]
    for k in range(1, TEAM):
        src = lax.rem(mate + k, TEAM)
        remote(
            fin_send.at[0], fin_recv.at[src], fsend.at[k], frecv.at[src], team * TEAM + src
        ).wait_recv()
    for m in range(TEAM):
        carry[m * part : (m + 1) * part] = fin_recv[m].astype(F32)

    reach_row = jnp.concatenate(
        [(tails[c] & (lasts[c] == last_seg)).astype(F32) for c in range(2)], axis=1
    )

    def unit_of(ref, u):
        u = 0 if u == last_tile else u
        return jnp.concatenate([ref[2 * u], ref[2 * u + 1]], axis=0)

    def sums_of(ref, u):
        return ref[2 * last_tile, u : u + 1, :] + ref[2 * last_tile + 1, u : u + 1, :]

    def outside(j):
        out = []
        for t in range(2):
            u = 2 * j + t
            lhs = left_side([unit_of(carry, u), unit_of(after, u)], [sums_of(carry, u), sums_of(after, u)])
            out.append(dot(lhs, qt[u * LANE : (u + 1) * LANE, :]))
        return out

    def close(j, parts):
        rows = []
        for t, res in enumerate(parts):
            u = 2 * j + t
            reach = jnp.broadcast_to(reach_row, (LANE, toks))
            numer = numt[u * LANE : (u + 1) * LANE, :] + res[:LANE] + reach * res[LANE : 2 * LANE]
            d_all = res[2 * LANE :]
            den = d_all[:PER] + d_all[PER : 2 * PER] + reach[:PER] * (d_all[2 * PER : 3 * PER] + d_all[3 * PER :])
            inv = 1.0 / (1.0 + dent[j, t * PER : (t + 1) * PER, :] + den)
            rows += [(numer[i * HDIM : (i + 1) * HDIM] * inv[i : i + 1]).astype(BF) for i in range(PER)]
        att[:, j * BLK : (j + 1) * BLK] = jnp.transpose(jnp.concatenate(rows, axis=0))

    held = outside(0)
    for j in range(1, groups):
        coming = outside(j)
        close(j - 1, held)
        held = coming
    close(groups - 1, held)

    ocopy.wait()
    square = jnp.zeros((toks, LANE), F32)

    def rise(b):
        end = min(b + BLK, d)
        if d - b > BLK:
            return dot(att[...], wo[:, b:end])
        return jnp.concatenate([dot(att[:chunk, :], wo[:, b:end]), dot(att[chunk:, :], wo[:, b:end])], axis=0)

    def settle(b, part_sum, square):
        end = min(b + BLK, d)
        mixed = hid[:, b:end].astype(F32) + part_sum
        sq = mixed * mixed
        for x in range(0, end - b, LANE):
            width = min(LANE, end - b - x)
            piece = sq[:, x : x + width]
            if width < LANE:
                piece = jnp.concatenate([piece, jnp.zeros((toks, LANE - width), F32)], axis=1)
            square = square + piece
        ybuf[:, b:end] = (mixed * jnp.broadcast_to(gain[b:end][None, :], mixed.shape)).astype(BF)
        return square

    for b in range(0, d, BLK):
        square = settle(b, rise(b), square)
    vel = dot(ybuf[...], vwt[...])
    meansq = jnp.sum(square, axis=1, keepdims=True) * (1.0 / d)
    lat = noisy_t[...] - vel * (0.5 * lax.rsqrt(meansq + 1e-06))
    noisy_t[...] = lat
    sorted_lat = dot(onehot[...], lat.astype(BF))
    dense = sorted_lat[:packed]
    for a in range(1, PER):
        dense = dense + pltpu.roll(sorted_lat[a * packed : (a + 1) * packed], a * HDIM, 1)
    outgoing[1 : n + 1] = dense.reshape(n, rows_to, LANE).astype(BF)

    def flip(k):
        to, bit = 0, 1
        while bit < n:
            have = lax.rem(me // bit, 2)
            to = to + bit * (1 - have if k & bit else have)
            bit *= 2
        return to

    def out_copy(k):
        to = flip(k)
        return remote(outgoing.at[pl.ds(to, 3)], incoming.at[me], asend.at[k], arecv.at[me], to)

    for k in range(n - 1, 0, -1):
        out_copy(k).start()
    incoming[me] = outgoing[pl.ds(me, 3)]
    lat_out[...] = jnp.transpose(noisy_t[...])[:HDIM]
    for k in range(1, n):
        src = flip(k)
        remote(outgoing.at[pl.ds(0, 3)], incoming.at[src], asend.at[k], arecv.at[src], src).wait_recv()

    for x in range(3):
        dense = incoming[:, x].astype(F32).reshape(packed, LANE)
        slots = [dense] + [pltpu.roll(dense, LANE - a * HDIM, 1) for a in range(1, PER)]
        at = slice(starts[x], starts[x] + sizes[x])
        wide[at, :] = dot(place[at, :], jnp.concatenate(slots, axis=0).astype(BF))

    ext = toks + 2 * edge
    x = wide[...]
    column = lax.rem(iota((ext, 128), 0), IW)
    lane = iota((ext, 128), 1)
    left = jnp.where(column == 0, 0.0, pltpu.roll(x, 1, 0))
    right = jnp.where(column == IW - 1, 0.0, pltpu.roll(x, ext - 1, 0))
    three = jnp.where(
        lane < HDIM, left,
        jnp.where(lane < 2 * HDIM, pltpu.roll(x, HDIM, 1),
                  jnp.where(lane < 3 * HDIM, pltpu.roll(right, 2 * HDIM, 1), 0.0)),
    )
    three = three.astype(BF)
    mid = toks + 2 * IW
    k3 = 3 * HDIM
    acc = dot(three[0:mid, :k3], w1[0])
    acc = acc + dot(three[IW : IW + mid, :k3], w1[1])
    acc = acc + dot(three[2 * IW : 2 * IW + mid, :k3], w1[2])
    feat = acc / (1.0 + jnp.exp(-acc))
    row_at = iota((mid, 1), 0) // IW
    outside = ((row_at == 0) & (me == 0)) | ((row_at == mid // IW - 1) & (me == n - 1))
    feat = jnp.where(outside, 0.0, feat).astype(BF).astype(F32)
    column = lax.rem(iota((mid, 1), 0), IW)
    shifted[1] = feat.astype(BF)
    shifted[0] = jnp.where(column == 0, 0.0, pltpu.roll(feat, 1, 0)).astype(BF)
    shifted[2] = jnp.where(column == IW - 1, 0.0, pltpu.roll(feat, mid - 1, 0)).astype(BF)
    w2copy.wait()
    out = None
    for a in range(3):
        for b in range(3):
            piece = dot(shifted[b, a * IW : a * IW + toks, :], w2[3 * a + b])
            out = piece if out is None else out + piece
    dec_out[...] = out.astype(BF)

    for k in range(1, TEAM):
        part_copy(k).wait_send()
        fin_copy(k).wait_send()

    for k in range(2):

        @pl.when(me >= k + 1)
        def _(k=k):
            lead_copy(k).wait_send()

    for to in range(1, teams):

        @pl.when(team < to)
        def _(to=to):
            plane_copy(to).wait_send()

    for k in range(1, n):
        out_copy(k).wait_send()


def flush(lat, dec, lat_out, dec_out, sem):
    copies = [
        pltpu.make_async_copy(dec, dec_out, sem.at[0]),
        pltpu.make_async_copy(lat, lat_out, sem.at[1]),
    ]
    for copy in copies:
        copy.start()
    for copy in copies:
        copy.wait()


def body(
    hidden_in, noisy_latents, span_ids, tile_map, qkv_weight, out_weight,
    norm_gain, velocity_weight, conv_first, conv_second,
):
    toks, d = hidden_in.shape
    inner = out_weight.shape[0]
    n = lax.axis_size("span")
    ch = conv_first.shape[3]
    chunk = toks // 2
    lo = inner // BLK
    koff = inner - lo * BLK
    kw = -(-(koff + inner) // BLK) * BLK
    tiles = kw // LANE
    units = -(-2 * tiles // TEAM) * TEAM // 2
    part = 2 * units // TEAM
    teams = n // TEAM
    edge = 2 * IW
    mid = toks + 2 * IW
    blocks = -(-qkv_weight.shape[1] // BLK)
    vm, dma = pltpu.VMEM, pltpu.SemaphoreType.DMA
    any_, vmem = pl.BlockSpec(memory_space=pl.ANY), pl.BlockSpec(memory_space=pltpu.VMEM)
    maps = tile_map.shape[0]
    half = HDIM // 2
    rows_to = toks // n // PER
    scratch = [
        vm((HDIM, toks), F32), vm((1, toks), jnp.int32), vm((1, maps), jnp.int32),
        vm((d,), F32), vm((HDIM, d), BF), vm((3, 3 * HDIM, ch), BF),
        vm((d, toks), BF), vm((toks, d), BF), vm(qkv_weight.shape, BF), vm((kw, d), BF),
        vm((9, ch, ch), BF),
        vm((kw, toks), BF), vm((toks, kw), BF), vm((kw, toks), BF),
        vm((kw, toks), F32), vm((kw // BLK, 8, toks), F32), vm((2, chunk, chunk), BF),
        vm((toks, kw), BF), vm((toks, d), BF), vm((d, LANE), BF),
        vm((tiles, HDIM, LANE), F32), vm((tiles, HDIM, LANE), F32),
        vm((tiles, HDIM, LANE), F32), vm((tiles, HDIM, LANE), F32),
        vm((2, half, LANE), F32), vm((2, half, LANE), F32),
        vm((2 * units, half, LANE), BF), vm((2 * units, half, LANE), BF), vm((2, 2 * units, half, LANE), BF),
        vm((TEAM, part, half, LANE), BF), vm((part, half, LANE), BF), vm((teams, part, half, LANE), BF),
        vm((TEAM, part, half, LANE), BF), vm((TEAM, part, half, LANE), BF),
        vm((part, half, LANE), F32), vm((2 * units, half, LANE), F32), vm((2 * units, half, LANE), F32),
        vm((toks, toks), BF), vm((n, toks), jnp.int32), vm((toks + 2 * edge, toks), BF), vm((toks, LANE), F32),
        vm((n + 2, rows_to, LANE), BF), vm((n, 3, rows_to, LANE), BF),
        vm((toks + 2 * edge, 128), F32),
        vm((3, mid, ch), BF),
        dma((blocks,)), dma((3,)), dma((toks // LANE,)), dma((6,)), dma((TEAM,)), dma((TEAM,)), dma((teams,)), dma((teams,)),
        dma((TEAM,)), dma((TEAM,)),
        dma((2,)), dma((2,)), dma((n,)), dma((n,)),
    ]
    latents, decoded = pl.pallas_call(
        functools.partial(kernel, (n, toks, d, inner)),
        out_shape=(
            pltpu.VMEM(noisy_latents.shape[::-1], F32),
            pltpu.VMEM((toks, ch), BF),
        ),
        in_specs=[any_] * 10,
        out_specs=(vmem, vmem),
        scratch_shapes=scratch,
        compiler_params=pltpu.CompilerParams(
            collective_id=0, has_side_effects=True, vmem_limit_bytes=60 * 1024 * 1024
        ),
    )(
        hidden_in.T, noisy_latents.T, span_ids.reshape(1, toks), tile_map.reshape(1, -1),
        qkv_weight, out_weight, norm_gain, velocity_weight.T,
        conv_first.reshape(3, 3 * HDIM, ch), conv_second.reshape(9, ch, ch),
    )
    latents, decoded = [pltpu.with_memory_space_constraint(x, pltpu.VMEM) for x in (latents, decoded)]
    latents, decoded = pl.pallas_call(
        flush,
        out_shape=(
            jax.ShapeDtypeStruct(latents.shape, F32),
            jax.ShapeDtypeStruct(decoded.shape, BF),
        ),
        in_specs=[vmem, vmem],
        out_specs=(any_, any_),
        scratch_shapes=[dma((2,))],
    )(latents, decoded)
    return latents.T, decoded.reshape(toks // IW, IW, ch)


def solution(mesh):
    rows = P(("groups", "span"), None)
    placed = (rows, rows, P(("groups", "span")), P("groups")) + (P(),) * 6
    return jax.shard_map(
        body, mesh=mesh, in_specs=placed,
        out_specs=(rows, P(("groups", "span"), None, None)), check_vma=False,
    )
```

```python
import functools

import jax
import jax.numpy as jnp
from jax import lax
from jax.experimental import pallas as pl
from jax.experimental.pallas import tpu as pltpu
from jax.sharding import PartitionSpec as P

HDIM = 32
IW = 64
BLK = 256
LANE = 128
PER = LANE // HDIM
TEAM = 4
LAG = 3
AHEAD = 4
BF = jnp.bfloat16
F32 = jnp.float32


def dot(a, b):
    return jnp.dot(a, b, preferred_element_type=F32)


def dot_nt(a, b):
    return lax.dot_general(a, b, (((1,), (1,)), ((), ())), preferred_element_type=F32)


def iota(shape, axis):
    return lax.broadcasted_iota(jnp.int32, shape, axis)


def kernel(
    cfg,
    hid_hbm, noisy_hbm, span_hbm, map_hbm, wq_hbm, wo_hbm, gain_hbm, vw_hbm, w1_hbm, w2_hbm,
    lat_out, dec_out,
    noisy, span_ref, map_ref, gain, vw, w1,
    hidt, hid, wq, wo, w2, qt, kp, vt, numt, dent, keep, att, ybuf, vwt,
    st_c0, st_b0, st_all, st_lead, sum_c0, sum_b0, st_send, lead_send, lead_recv,
    part_recv, plane_send, plane_recv, fin_send, fin_recv, base, carry, after, onehot, map_rows, place, noisy_t, outgoing, incoming,
    wide, shifted,
    wsem, lsem, hsem, isem, psend, precv, gsend, grecv, fsend, frecv, lead_ssem, lead_rsem, asend, arecv,
):
    n, toks, d, inner = cfg
    me = lax.axis_index("span")
    mate = lax.rem(me, TEAM)
    team = me // TEAM
    teams = n // TEAM
    share = toks // n
    rows_to = share // PER
    chunk = toks // 2
    lo = inner // BLK
    koff = inner - lo * BLK
    kw = kp.shape[1]
    tiles = kw // LANE
    units = st_send.shape[0] // 2
    part = 2 * units // TEAM
    half = HDIM // 2
    heads = inner // HDIM
    first_slot = koff // HDIM
    last_slot = first_slot + heads

    def remote(src, dst, ss, rs, dev):
        return pltpu.make_async_remote_copy(
            src_ref=src, dst_ref=dst, send_sem=ss, recv_sem=rs,
            device_id={"span": dev}, device_id_type=pl.DeviceIdType.MESH,
        )

    total = wq_hbm.shape[1]
    full = total // BLK
    rest = total - full * BLK

    def wcopy(b):
        cols = slice(b * BLK, min(b * BLK + BLK, total))
        return pltpu.make_async_copy(wq_hbm.at[:, cols], wq.at[:, cols], wsem.at[b])

    def hcopy(i):
        cols = pl.ds(i * LANE if isinstance(i, int) else pl.multiple_of(i * LANE, LANE), LANE)
        return pltpu.make_async_copy(hid_hbm.at[:, cols], hidt.at[:, cols], hsem.at[i])

    for i in range(toks // LANE):
        hcopy(i).start()
    smalls = [
        pltpu.make_async_copy(src, dst, isem.at[i])
        for i, (src, dst) in enumerate([
            (span_hbm, span_ref), (vw_hbm, vw), (map_hbm, map_ref), (noisy_hbm, noisy),
            (gain_hbm, gain), (w1_hbm, w1),
        ])
    ]
    for copy in smalls[:2]:
        copy.start()
    ocopy = pltpu.make_async_copy(wo_hbm, wo.at[koff : koff + inner], lsem.at[1])
    w2copy = pltpu.make_async_copy(w2_hbm, w2, lsem.at[2])
    pending = [wcopy(full)] if rest else []
    pending += [wcopy(b) for b in range(lo, full)] + smalls[2:] + [wcopy(b) for b in range(lo)] + [ocopy, w2copy]

    def fetch(count):
        for copy in pending[:count]:
            copy.start()
        del pending[:count]

    fetch(AHEAD)

    barrier = pltpu.get_barrier_semaphore()
    for k in range(1, n):
        pl.semaphore_signal(
            barrier, inc=1, device_id={"span": lax.rem(me + k, n)},
            device_id_type=pl.DeviceIdType.MESH,
        )

    def clear(ref, row0, row1, dtype):
        if row1 > row0:
            ref[row0:row1, :] = jnp.zeros((row1 - row0, ref.shape[1]), dtype)

    for ref, dtype in ((qt, BF), (vt, BF), (numt, F32), (wo, BF)):
        clear(ref, 0, koff, dtype)
        clear(ref, koff + inner, kw, dtype)

    for j in (0, kw // BLK - 1):
        dent[j] = jnp.zeros((8, toks), F32)

    for copy in smalls[:2]:
        copy.wait()
    span_row = span_ref[...].astype(F32)
    span_col = jnp.transpose(jnp.broadcast_to(span_row, (LANE, toks)))[:, 0:1]
    first_seg = span_row[:, 0:1]
    last_seg = span_row[:, toks - 1 : toks]
    lasts = [span_row[:, (c + 1) * chunk - 1 : (c + 1) * chunk] for c in range(2)]
    for c in range(2):
        rs = slice(c * chunk, (c + 1) * chunk)
        sr = span_row[:, rs]
        keep[c] = ((span_col[rs, :] <= sr) & (sr < lasts[c])).astype(F32).astype(BF)
    vwt[...] = jnp.concatenate([jnp.transpose(vw[...]), jnp.zeros((d, LANE - HDIM), F32).astype(BF)], axis=1)

    def turn(i, c):
        cols = pl.ds(pl.multiple_of(i * LANE, LANE), LANE)
        hcopy(i).wait()
        hid[cols, :] = jnp.transpose(hidt[:, cols])
        return c

    lax.fori_loop(0, chunk // LANE, turn, 0)
    fetch(2)

    def finish(out, b, rs):
        begin, end = b * BLK, b * BLK + BLK
        if begin < 2 * inner:
            pos = jnp.maximum(out, jnp.zeros_like(out))
            if end > 2 * inner:
                pos = jnp.where(iota(out.shape, 1) < 2 * inner - begin, pos, out)
            out = pos
        if end > inner and begin < 2 * inner:
            kp[rs, begin - lo * BLK : end - lo * BLK] = out
        if begin < inner:
            rows = min(end, inner) - begin
            qt[koff + begin : koff + begin + rows, rs] = jnp.transpose(out)[:rows]
        if end > 2 * inner:
            skip = max(2 * inner - begin, 0)
            row = begin + skip - 2 * inner + koff
            vt[row : row + BLK - skip, rs] = jnp.transpose(out)[skip:]

    def project(blocks, ready=False, spans=None):
        if not ready:
            for b in blocks:
                wcopy(b).wait()
            fetch(3)
        for at, b in enumerate(blocks):
            cols = slice(b * BLK, b * BLK + BLK)
            pair = len(blocks) % 2 == 1 and at == len(blocks) - 1
            for rs in spans or ([slice(0, chunk), slice(chunk, toks)] if pair else [slice(0, toks)]):
                finish(dot(hid[rs, :], wq[:, cols]).astype(BF), b, rs)

    def project_rest():
        tail_w = jnp.transpose(wq[:, full * BLK : total])
        row = full * BLK - 2 * inner + koff
        vt[row : row + rest, :] = dot(tail_w, hidt[...]).astype(BF)

    early = list(range(lo, full))
    for at in range(0, len(early) - 1, 2):
        blocks = early[at : at + (2 if at + 3 < len(early) else 3)]
        if at > 0:
            project(blocks)
            continue
        for b in blocks + ([full] if rest else []):
            wcopy(b).wait()
        for i in range(chunk // LANE, toks // LANE):
            hcopy(i).wait()
        fetch(3)
        project(blocks, ready=True, spans=[slice(0, chunk)])
        for i in range(chunk // LANE, toks // LANE):
            rows = slice(i * LANE, (i + 1) * LANE)
            hid[rows, :] = jnp.transpose(hidt[:, rows])
        if rest:
            project_rest()
        project(blocks, ready=True, spans=[slice(chunk, toks)])
    for copy in smalls[2:]:
        copy.wait()

    ones16 = jnp.ones((16, chunk), F32).astype(BF)
    lead_row = (span_row == first_seg).astype(F32).astype(BF)
    b0_row = (span_row[:, chunk:] <= lasts[0]).astype(F32).astype(BF)
    lane_slot = iota((HDIM, LANE), 1) // HDIM

    def diag(res, t):
        parts = [res[(t * PER + i) * HDIM : (t * PER + i + 1) * HDIM, t * LANE : (t + 1) * LANE] for i in range(PER)]
        out = parts[PER - 1]
        for i in range(PER - 2, -1, -1):
            out = jnp.where(lane_slot == i, parts[i], out)
        return out

    at_tile = [slice(0, LANE), slice(LANE, BLK)]
    one = slice(BLK, BLK + 1)

    def sides(j, c):
        cols, rs = slice(j * BLK, (j + 1) * BLK), slice(c * chunk, (c + 1) * chunk)
        return jnp.concatenate([vt[cols, rs], ones16], axis=0), kp[rs, cols]

    for j in range(tiles // 2):
        c0, c1 = [dot(*sides(j, c)) for c in range(2)]
        for t in range(2):
            u = 2 * j + t
            s0 = diag(c0, t)
            st_c0[u] = s0
            st_all[u] = s0 + diag(c1, t)
            sum_c0[0, u : u + 1, :] = c0[one, at_tile[t]]
            sum_c0[1, u : u + 1, :] = c0[one, at_tile[t]] + c1[one, at_tile[t]]

    row_no = iota((half, LANE), 0)
    last_tile = tiles - 1

    def pack(dst, src, sums):
        for u in range(last_tile):
            full_unit = src[u] + src[last_tile] if u == 0 else src[u]
            for x in range(2):
                dst[2 * u + x] = full_unit[x * half : (x + 1) * half].astype(BF)
        sums = jnp.where(row_no < tiles, sums, 0.0)
        high = sums.astype(BF).astype(F32)
        low = sums - high
        high = jnp.where(row_no == half - 1, jnp.broadcast_to(first_seg, (half, LANE)), high)
        dst[2 * last_tile] = high.astype(BF)
        dst[2 * last_tile + 1] = low.astype(BF)
        for u in range(2 * tiles, 2 * units):
            dst[u] = jnp.zeros((half, LANE), F32).astype(BF)

    pack(st_send, st_all, sum_c0[1])

    pl.semaphore_wait(barrier, n - 1)

    def part_copy(k):
        to = lax.rem(mate + k, TEAM)
        return remote(
            st_send.at[pl.ds(part * to, part)], part_recv.at[mate],
            psend.at[k], precv.at[mate], team * TEAM + to,
        )

    for k in range(1, TEAM):
        part_copy(k).start()

    def lead_copy(k):
        return remote(
            lead_send, lead_recv.at[k], lead_ssem.at[k], lead_rsem.at[k],
            lax.rem(me - 1 - k + n, n),
        )

    for j in range(tiles // 2):
        (v0, k0), (v1, k1) = sides(j, 0), sides(j, 1)
        l0, l1 = dot(v0 * lead_row[:, :chunk], k0), dot(v1 * lead_row[:, chunk:], k1)
        b0 = dot(v1 * b0_row, k1)
        for t in range(2):
            u = 2 * j + t
            st_b0[u] = st_c0[u] + diag(b0, t)
            st_lead[u] = diag(l0, t) + diag(l1, t)
            sum_b0[0, u : u + 1, :] = sum_c0[0, u : u + 1, :] + b0[one, at_tile[t]]
            sum_b0[1, u : u + 1, :] = l0[one, at_tile[t]] + l1[one, at_tile[t]]

    pack(lead_send, st_lead, sum_b0[1])

    fetch(len(pending))
    for b in range(lo // 2):
        wcopy(b).wait()
    mine = map_ref[:, pl.ds(pl.multiple_of(me * toks, toks), toks)]
    target = mine // toks
    for b in range(n):
        map_rows[b : b + 1, :] = map_ref[:, b * toks : (b + 1) * toks]
    goal = map_rows[...] // toks
    where_in = map_rows[...] - goal * toks
    hits = [iota((n, toks), 0) == jnp.broadcast_to(target, (n, toks))]
    hits += [goal == me - 1 + x for x in range(3)]
    upper = (iota((toks, toks), 0) <= iota((toks, toks), 1)).astype(BF)
    cum = dot(jnp.concatenate([h.astype(F32) for h in hits], axis=0).astype(BF), upper)
    rank = jnp.sum(jnp.where(hits[0], cum[:n], 0.0), axis=0, keepdims=True).astype(jnp.int32) - 1
    packed = n * rows_to
    slot = rank // rows_to * packed + target * rows_to + lax.rem(rank, rows_to)
    onehot[...] = (iota((toks, toks), 0) == jnp.broadcast_to(slot, (toks, toks))).astype(F32).astype(BF)
    project(list(range(lo // 2)), ready=True)
    spot_f = where_in.astype(F32)
    lane_n = iota((n, LANE), 1)
    found = []
    for x in range(3):
        order = jnp.where(hits[1 + x], cum[n * (1 + x) : n * (2 + x)], 0.0)
        table = jnp.zeros((n, LANE), F32)
        for r in range(share):
            one = jnp.sum(jnp.where(order == float(r + 1), spot_f, 0.0), axis=1, keepdims=True)
            table = jnp.where(lane_n == r, one, table)
        whole_pos = table.astype(jnp.int32)
        found.append((whole_pos // IW).astype(F32))
        found.append(lax.rem(whole_pos, IW).astype(F32))
    slot_no = iota((LANE, toks), 1)
    rank_of = slot_no // packed * rows_to + lax.rem(slot_no, rows_to)
    spread = (iota((LANE, toks), 0) == rank_of).astype(F32).astype(BF)
    filled = dot(jnp.concatenate(found, axis=0).astype(BF), spread)
    source = lax.rem(iota((n, toks), 1), packed) // rows_to
    owned = iota((n, toks), 0) == source
    edge = 2 * IW
    starts = (0, edge, edge + toks)
    sizes = (edge, toks, edge)
    for x in range(3):
        lines, spots = [
            jnp.sum(jnp.where(owned, filled[n * (2 * x + y) : n * (2 * x + y + 1)], 0.0), axis=0, keepdims=True)
            for y in range(2)
        ]
        pos = (lines * float(IW) + spots).astype(jnp.int32)
        if x == 0:
            pos = pos - (toks - edge)
        place[starts[x] : starts[x] + sizes[x], :] = (
            iota((sizes[x], toks), 0) == jnp.broadcast_to(pos, (sizes[x], toks))
        ).astype(F32).astype(BF)
    for x in (0, n + 1):
        outgoing[x] = jnp.zeros((rows_to, LANE), F32).astype(BF)
    noisy_t[...] = jnp.concatenate(
        [jnp.transpose(noisy[...]), jnp.zeros((toks, LANE - HDIM), F32)], axis=1
    )

    part_recv[mate] = st_send[pl.ds(part * mate, part)]
    for k in range(1, TEAM):
        src = lax.rem(mate + k, TEAM)
        remote(
            st_send.at[pl.ds(0, part)], part_recv.at[src], psend.at[k], precv.at[src], team * TEAM + src
        ).wait_recv()
    whole = part_recv[0].astype(F32)
    for src in range(1, TEAM):
        whole = whole + part_recv[src].astype(F32)
    plane_send[...] = whole.astype(BF)

    def plane_copy(to):
        return remote(
            plane_send, plane_recv.at[team], gsend.at[to], grecv.at[team], TEAM * to + mate
        )

    for to in range(teams - 1, 0, -1):

        @pl.when(team < to)
        def _(to=to):
            plane_copy(to).start()

    for k in range(2):

        @pl.when(me >= k + 1)
        def _(k=k):
            lead_copy(k).start()

    project(list(range(lo // 2, lo)))

    def attend(jobs):
        def place(j, s):
            t, i = s // PER, s % PER
            if isinstance(j, int):
                return pl.ds(j * BLK + s * HDIM, HDIM), pl.ds(j * BLK + t * LANE, LANE), i
            return (
                pl.ds(pl.multiple_of(j * BLK + s * HDIM, HDIM), HDIM),
                pl.ds(pl.multiple_of(j * BLK + t * LANE, LANE), LANE), i,
            )

        def scores(j, s, c):
            rs = slice(c * chunk, (c + 1) * chunk)
            head, tile, i = place(j, s)
            pieces = [qt[head, rs]]
            if i:
                pieces = [jnp.zeros((i * HDIM, chunk), BF)] + pieces
            if i < PER - 1:
                pieces = pieces + [jnp.zeros(((PER - 1 - i) * HDIM, chunk), BF)]
            return dot(kp[rs, tile], jnp.concatenate(pieces, axis=0)).astype(BF) * keep[c]

        def values(j, s, c, score):
            rs = slice(c * chunk, (c + 1) * chunk)
            head, _, _ = place(j, s)
            out = dot(jnp.concatenate([vt[head, rs], ones16], axis=0), score)
            numt[head, rs] = out[:HDIM]
            dent[j, s : s + 1, rs] = out[HDIM : HDIM + 1]

        queue = []
        for job in jobs:
            queue.append((job, scores(*job)))
            if len(queue) > LAG:
                old, score = queue.pop(0)
                values(*old, score)
        for old, score in queue:
            values(*old, score)

    slots_of = BLK // HDIM
    groups = kw // BLK
    plain, extra = [], []
    for j in range(groups):
        slots = [s for s in range(slots_of) if first_slot <= j * slots_of + s < last_slot]
        if len(slots) == slots_of:
            plain.append(j)
        else:
            extra += [(j, s, c) for s in slots for c in range(2)]
    attend(extra)

    def attend_loop(j, carry_in):
        attend([(j, s, c) for s in range(slots_of) for c in range(2)])
        return carry_in

    lax.fori_loop(plain[0], plain[-1], attend_loop, 0)

    base[...] = jnp.zeros_like(base)
    for src in range(teams - 1):

        @pl.when(src < team)
        def _(src=src):
            remote(
                plane_send, plane_recv.at[src], gsend.at[src], grecv.at[src], TEAM * src + mate
            ).wait_recv()
            base[...] = base[...] + plane_recv[src].astype(F32)

    run = base[...]
    for m in range(TEAM):
        fin_send[m] = run.astype(BF)
        if m < TEAM - 1:
            run = run + part_recv[m].astype(F32)

    def fin_copy(k):
        to = lax.rem(mate + k, TEAM)
        return remote(
            fin_send.at[to], fin_recv.at[mate], fsend.at[k], frecv.at[mate], team * TEAM + to
        )

    for k in range(1, TEAM):
        fin_copy(k).start()

    lax.fori_loop(plain[-1], plain[-1] + 1, attend_loop, 0)

    tails = [span_row[:, c * chunk : (c + 1) * chunk] == lasts[c] for c in range(2)]
    masks = [(lane_slot == i).astype(F32).astype(BF) for i in range(PER)]
    den_slot = iota((half, LANE), 0)
    den_live = lax.rem(den_slot, PER) == iota((half, LANE), 1) // HDIM

    def left_side(states, sums):
        rows = []
        for state in states:
            state = state.astype(BF)
            rows += [state * m for m in masks]
        levels = []
        for total_sum in sums:
            high = total_sum.astype(BF).astype(F32)
            levels += [high, total_sum - high]
        den = jnp.broadcast_to(levels[-1], (half, LANE))
        for x in range(len(levels) - 2, -1, -1):
            den = jnp.where(den_slot < PER * (x + 1), levels[x], den)
        live = den_live & (den_slot < PER * len(levels))
        return jnp.concatenate(rows + [jnp.where(live, den, 0.0).astype(BF)], axis=0)

    def inside(j, carry_in):
        work = []
        for t in range(2):
            u = 2 * j + t
            tile = pl.ds(pl.multiple_of(j * BLK + t * LANE, LANE), LANE)
            one = pl.ds(u, 1)
            lhs = [
                left_side([st_b0[u]], [sum_b0[0, one, :]]),
                left_side([st_c0[u], st_all[u]], [sum_c0[0, one, :], sum_c0[1, one, :]]),
            ]
            for c in range(2):
                rs = slice(c * chunk, (c + 1) * chunk)
                work.append((t, c, tile, rs, dot(lhs[c], qt[tile, rs])))
        for t, c, tile, rs, res in work:
            tail = jnp.broadcast_to(tails[c], (LANE, chunk))
            d_all = res[LANE * (c + 1) :]
            d_one = d_all[:PER] + d_all[PER : 2 * PER]
            if c == 0:
                more, d_more = jnp.where(tail, res[:LANE], 0.0), jnp.where(tail[:PER], d_one, 0.0)
            else:
                d_two = d_all[2 * PER : 3 * PER] + d_all[3 * PER :]
                more, d_more = jnp.where(tail, res[LANE : 2 * LANE], res[:LANE]), jnp.where(tail[:PER], d_two, d_one)
            numt[tile, rs] = numt[tile, rs] + more
            dent[j, t * PER : (t + 1) * PER, rs] = dent[j, t * PER : (t + 1) * PER, rs] + d_more
        return carry_in

    lax.fori_loop(0, groups, inside, 0)

    after[...] = jnp.zeros_like(after)
    for k in range(2):

        @pl.when(me + 1 + k < n)
        def _(k=k):
            remote(
                lead_send, lead_recv.at[k], lead_ssem.at[k], lead_rsem.at[k], lax.rem(me + 1 + k, n)
            ).wait_recv()
            same = (lead_recv[k, 2 * last_tile, half - 1 : half, 0:1].astype(F32) == last_seg).astype(F32)
            after[...] = after[...] + lead_recv[k].astype(F32) * same

    fin_recv[mate] = fin_send[mate]
    for k in range(1, TEAM):
        src = lax.rem(mate + k, TEAM)
        remote(
            fin_send.at[0], fin_recv.at[src], fsend.at[k], frecv.at[src], team * TEAM + src
        ).wait_recv()
    for m in range(TEAM):
        carry[m * part : (m + 1) * part] = fin_recv[m].astype(F32)

    reach_row = jnp.concatenate(
        [(tails[c] & (lasts[c] == last_seg)).astype(F32) for c in range(2)], axis=1
    )

    def unit_of(ref, u):
        u = 0 if u == last_tile else u
        return jnp.concatenate([ref[2 * u], ref[2 * u + 1]], axis=0)

    def sums_of(ref, u):
        return ref[2 * last_tile, u : u + 1, :] + ref[2 * last_tile + 1, u : u + 1, :]

    def outside(j):
        out = []
        for t in range(2):
            u = 2 * j + t
            lhs = left_side([unit_of(carry, u), unit_of(after, u)], [sums_of(carry, u), sums_of(after, u)])
            out.append(dot(lhs, qt[u * LANE : (u + 1) * LANE, :]))
        return out

    def close(j, parts):
        rows = []
        for t, res in enumerate(parts):
            u = 2 * j + t
            reach = jnp.broadcast_to(reach_row, (LANE, toks))
            numer = numt[u * LANE : (u + 1) * LANE, :] + res[:LANE] + reach * res[LANE : 2 * LANE]
            d_all = res[2 * LANE :]
            den = d_all[:PER] + d_all[PER : 2 * PER] + reach[:PER] * (d_all[2 * PER : 3 * PER] + d_all[3 * PER :])
            inv = 1.0 / (1.0 + dent[j, t * PER : (t + 1) * PER, :] + den)
            rows += [(numer[i * HDIM : (i + 1) * HDIM] * inv[i : i + 1]).astype(BF) for i in range(PER)]
        att[:, j * BLK : (j + 1) * BLK] = jnp.transpose(jnp.concatenate(rows, axis=0))

    held = outside(0)
    for j in range(1, groups):
        coming = outside(j)
        close(j - 1, held)
        held = coming
    close(groups - 1, held)

    ocopy.wait()
    square = jnp.zeros((toks, LANE), F32)

    def rise(b):
        end = min(b + BLK, d)
        if d - b > BLK:
            return dot(att[...], wo[:, b:end])
        return jnp.concatenate([dot(att[:chunk, :], wo[:, b:end]), dot(att[chunk:, :], wo[:, b:end])], axis=0)

    def settle(b, part_sum, square):
        end = min(b + BLK, d)
        mixed = hid[:, b:end].astype(F32) + part_sum
        sq = mixed * mixed
        for x in range(0, end - b, LANE):
            width = min(LANE, end - b - x)
            piece = sq[:, x : x + width]
            if width < LANE:
                piece = jnp.concatenate([piece, jnp.zeros((toks, LANE - width), F32)], axis=1)
            square = square + piece
        ybuf[:, b:end] = (mixed * jnp.broadcast_to(gain[b:end][None, :], mixed.shape)).astype(BF)
        return square

    vel = jnp.zeros((toks, LANE), F32)
    done = 0
    for b in range(0, d, BLK):
        part_sum = rise(b)
        if b - done >= 4 * BLK:
            vel = vel + dot(ybuf[:, done:b], vwt[done:b, :])
            done = b
        square = settle(b, part_sum, square)
    vel = vel + dot(ybuf[:, done:], vwt[done:, :])
    meansq = jnp.sum(square, axis=1, keepdims=True) * (1.0 / d)
    lat = noisy_t[...] - vel * (0.5 * lax.rsqrt(meansq + 1e-06))
    noisy_t[...] = lat
    sorted_lat = dot(onehot[...], lat.astype(BF))
    dense = sorted_lat[:packed]
    for a in range(1, PER):
        dense = dense + pltpu.roll(sorted_lat[a * packed : (a + 1) * packed], a * HDIM, 1)
    outgoing[1 : n + 1] = dense.reshape(n, rows_to, LANE).astype(BF)

    def flip(k):
        to, bit = 0, 1
        while bit < n:
            have = lax.rem(me // bit, 2)
            to = to + bit * (1 - have if k & bit else have)
            bit *= 2
        return to

    def out_copy(k):
        to = flip(k)
        return remote(outgoing.at[pl.ds(to, 3)], incoming.at[me], asend.at[k], arecv.at[me], to)

    for k in range(n - 1, 0, -1):
        out_copy(k).start()
    incoming[me] = outgoing[pl.ds(me, 3)]
    lat_out[...] = jnp.transpose(noisy_t[...])[:HDIM]
    for k in range(1, n):
        src = flip(k)
        remote(outgoing.at[pl.ds(0, 3)], incoming.at[src], asend.at[k], arecv.at[src], src).wait_recv()

    for x in range(3):
        dense = incoming[:, x].astype(F32).reshape(packed, LANE)
        slots = [dense] + [pltpu.roll(dense, LANE - a * HDIM, 1) for a in range(1, PER)]
        at = slice(starts[x], starts[x] + sizes[x])
        wide[at, :] = dot(place[at, :], jnp.concatenate(slots, axis=0).astype(BF))

    ext = toks + 2 * edge
    x = wide[...]
    column = lax.rem(iota((ext, 128), 0), IW)
    lane = iota((ext, 128), 1)
    left = jnp.where(column == 0, 0.0, pltpu.roll(x, 1, 0))
    right = jnp.where(column == IW - 1, 0.0, pltpu.roll(x, ext - 1, 0))
    three = jnp.where(
        lane < HDIM, left,
        jnp.where(lane < 2 * HDIM, pltpu.roll(x, HDIM, 1),
                  jnp.where(lane < 3 * HDIM, pltpu.roll(right, 2 * HDIM, 1), 0.0)),
    )
    three = three.astype(BF)
    mid = toks + 2 * IW
    k3 = 3 * HDIM
    acc = dot(three[0:mid, :k3], w1[0])
    acc = acc + dot(three[IW : IW + mid, :k3], w1[1])
    acc = acc + dot(three[2 * IW : 2 * IW + mid, :k3], w1[2])
    feat = acc / (1.0 + jnp.exp(-acc))
    row_at = iota((mid, 1), 0) // IW
    outside = ((row_at == 0) & (me == 0)) | ((row_at == mid // IW - 1) & (me == n - 1))
    feat = jnp.where(outside, 0.0, feat).astype(BF).astype(F32)
    column = lax.rem(iota((mid, 1), 0), IW)
    shifted[1] = feat.astype(BF)
    shifted[0] = jnp.where(column == 0, 0.0, pltpu.roll(feat, 1, 0)).astype(BF)
    shifted[2] = jnp.where(column == IW - 1, 0.0, pltpu.roll(feat, mid - 1, 0)).astype(BF)
    w2copy.wait()
    out = None
    for a in range(3):
        for b in range(3):
            piece = dot(shifted[b, a * IW : a * IW + toks, :], w2[3 * a + b])
            out = piece if out is None else out + piece
    dec_out[...] = out.astype(BF)

    for k in range(1, TEAM):
        part_copy(k).wait_send()
        fin_copy(k).wait_send()

    for k in range(2):

        @pl.when(me >= k + 1)
        def _(k=k):
            lead_copy(k).wait_send()

    for to in range(1, teams):

        @pl.when(team < to)
        def _(to=to):
            plane_copy(to).wait_send()

    for k in range(1, n):
        out_copy(k).wait_send()


def flush(lat, dec, lat_out, dec_out, sem):
    copies = [
        pltpu.make_async_copy(dec, dec_out, sem.at[0]),
        pltpu.make_async_copy(lat, lat_out, sem.at[1]),
    ]
    for copy in copies:
        copy.start()
    for copy in copies:
        copy.wait()


def body(
    hidden_in, noisy_latents, span_ids, tile_map, qkv_weight, out_weight,
    norm_gain, velocity_weight, conv_first, conv_second,
):
    toks, d = hidden_in.shape
    inner = out_weight.shape[0]
    n = lax.axis_size("span")
    ch = conv_first.shape[3]
    chunk = toks // 2
    lo = inner // BLK
    koff = inner - lo * BLK
    kw = -(-(koff + inner) // BLK) * BLK
    tiles = kw // LANE
    units = -(-2 * tiles // TEAM) * TEAM // 2
    part = 2 * units // TEAM
    teams = n // TEAM
    edge = 2 * IW
    mid = toks + 2 * IW
    blocks = -(-qkv_weight.shape[1] // BLK)
    vm, dma = pltpu.VMEM, pltpu.SemaphoreType.DMA
    any_, vmem = pl.BlockSpec(memory_space=pl.ANY), pl.BlockSpec(memory_space=pltpu.VMEM)
    maps = tile_map.shape[0]
    half = HDIM // 2
    rows_to = toks // n // PER
    scratch = [
        vm((HDIM, toks), F32), vm((1, toks), jnp.int32), vm((1, maps), jnp.int32),
        vm((d,), F32), vm((HDIM, d), BF), vm((3, 3 * HDIM, ch), BF),
        vm((d, toks), BF), vm((toks, d), BF), vm(qkv_weight.shape, BF), vm((kw, d), BF),
        vm((9, ch, ch), BF),
        vm((kw, toks), BF), vm((toks, kw), BF), vm((kw, toks), BF),
        vm((kw, toks), F32), vm((kw // BLK, 8, toks), F32), vm((2, chunk, chunk), BF),
        vm((toks, kw), BF), vm((toks, d), BF), vm((d, LANE), BF),
        vm((tiles, HDIM, LANE), F32), vm((tiles, HDIM, LANE), F32),
        vm((tiles, HDIM, LANE), F32), vm((tiles, HDIM, LANE), F32),
        vm((2, half, LANE), F32), vm((2, half, LANE), F32),
        vm((2 * units, half, LANE), BF), vm((2 * units, half, LANE), BF), vm((2, 2 * units, half, LANE), BF),
        vm((TEAM, part, half, LANE), BF), vm((part, half, LANE), BF), vm((teams, part, half, LANE), BF),
        vm((TEAM, part, half, LANE), BF), vm((TEAM, part, half, LANE), BF),
        vm((part, half, LANE), F32), vm((2 * units, half, LANE), F32), vm((2 * units, half, LANE), F32),
        vm((toks, toks), BF), vm((n, toks), jnp.int32), vm((toks + 2 * edge, toks), BF), vm((toks, LANE), F32),
        vm((n + 2, rows_to, LANE), BF), vm((n, 3, rows_to, LANE), BF),
        vm((toks + 2 * edge, 128), F32),
        vm((3, mid, ch), BF),
        dma((blocks,)), dma((3,)), dma((toks // LANE,)), dma((6,)), dma((TEAM,)), dma((TEAM,)), dma((teams,)), dma((teams,)),
        dma((TEAM,)), dma((TEAM,)),
        dma((2,)), dma((2,)), dma((n,)), dma((n,)),
    ]
    latents, decoded = pl.pallas_call(
        functools.partial(kernel, (n, toks, d, inner)),
        out_shape=(
            pltpu.VMEM(noisy_latents.shape[::-1], F32),
            pltpu.VMEM((toks, ch), BF),
        ),
        in_specs=[any_] * 10,
        out_specs=(vmem, vmem),
        scratch_shapes=scratch,
        compiler_params=pltpu.CompilerParams(
            collective_id=0, has_side_effects=True, vmem_limit_bytes=60 * 1024 * 1024
        ),
    )(
        hidden_in.T, noisy_latents.T, span_ids.reshape(1, toks), tile_map.reshape(1, -1),
        qkv_weight, out_weight, norm_gain, velocity_weight.T,
        conv_first.reshape(3, 3 * HDIM, ch), conv_second.reshape(9, ch, ch),
    )
    latents, decoded = [pltpu.with_memory_space_constraint(x, pltpu.VMEM) for x in (latents, decoded)]
    latents, decoded = pl.pallas_call(
        flush,
        out_shape=(
            jax.ShapeDtypeStruct(latents.shape, F32),
            jax.ShapeDtypeStruct(decoded.shape, BF),
        ),
        in_specs=[vmem, vmem],
        out_specs=(any_, any_),
        scratch_shapes=[dma((2,))],
    )(latents, decoded)
    return latents.T, decoded.reshape(toks // IW, IW, ch)


def solution(mesh):
    rows = P(("groups", "span"), None)
    placed = (rows, rows, P(("groups", "span")), P("groups")) + (P(),) * 6
    return jax.shard_map(
        body, mesh=mesh, in_specs=placed,
        out_specs=(rows, P(("groups", "span"), None, None)), check_vma=False,
    )
```
